32 devices in a mesh: seq: 16 (over z, x, core), tensor: 2 (over y).
Axes of the slice: x: 2, y: 2, z: 4, core: 2. Of those that a mesh axis runs over, the one named last changes fastest.
Arguments:
- hidden: bfloat16 [3072, 4096], P('seq', 'tensor'), may hold values from -170 to 170
- depth: int32 [3072], P('seq'), may hold values from 0 to 4, as said below
- norm_gain: float32 [4096], replicated, may hold values from 0.5 to 2
- w_query: bfloat16 [4096, 2048], P('seq', 'tensor'), may hold values from -2.5 to 2.5
- w_key: bfloat16 [4096, 1024], P('seq', 'tensor'), may hold values from -1 to 1
- w_value: bfloat16 [4096, 1024], P('seq', 'tensor'), may hold values from -0.09375 to 0.09375
- w_out: bfloat16 [2048, 4096], P('tensor', 'seq'), may hold values from -0.1875 to 0.1875
Outputs:
- mixed: bfloat16 [3072, 4096], P('seq', 'tensor')
The draws below stay inside these ranges and needn't reach their ends.
Inputs may be any that keep to these rules, and one draw needn't show every extreme that they name: A token takes part in this step when its depth exceeds 2. In each aligned block of 192 tokens at most 96 take part, and some block holds exactly 96.
All inputs are finite; a program needn't handle non-finite values.
Results may differ from the reference program's by a relative error of at most 0.015.
Values may be sent and summed in bfloat16 or wider, within the bound.
A program may use at most 64 MiB of HBM per device.

```python
import math
import jax
import jax.numpy as jnp
from jax import lax

D = 4096
HD = 128
KVH = 8
QH = 16
STEP = 2
TOK_DEV = 192
CAP = 96
DOCUMENT_TOKENS = 3072
N_TENSOR = 2


def permuted(subkey):
    return jax.random.permutation(subkey, TOK_DEV)


def continuing_tokens(key):
    blocks = DOCUMENT_TOKENS // TOK_DEV
    subkeys = jax.random.split(jax.random.fold_in(key, 101), 2)
    block_ids = jnp.arange(blocks, dtype=jnp.int32)
    ceiling = CAP * (block_ids + 1) // blocks
    counts = jax.random.randint(subkeys[0], (blocks,), 0, ceiling + 1)
    counts = jnp.where(block_ids == blocks - 1, CAP, counts)
    ranked_tokens = jax.vmap(permuted)(jax.random.split(subkeys[1], blocks))
    chosen_tokens = ranked_tokens < counts[:, None]
    return chosen_tokens


def draw_depth(key, part):
    chosen_tokens = continuing_tokens(key)
    subkeys = jax.random.split(jax.random.fold_in(key, 202), 2)
    higher = jax.random.randint(subkeys[0], chosen_tokens.shape, STEP + 1, 5)
    lower = jax.random.randint(subkeys[1], chosen_tokens.shape, 0, STEP + 1)
    return jnp.where(chosen_tokens, higher, lower).reshape(DOCUMENT_TOKENS).astype(jnp.int32)


def draw_norm_gain(key, part):
    values = jax.random.uniform(jax.random.fold_in(key, 404), (D,), jnp.float32, 0.5, 1.5)
    return values.astype(jnp.float32)


def draw_w_query(key, part):
    spread = (8.0 / D) ** 0.5
    values = jax.random.normal(jax.random.fold_in(key, 414), (D, QH * HD), jnp.float32) * spread
    values = jnp.clip(values, -6.0 * spread, 6.0 * spread)
    return values.astype(jnp.bfloat16)


def draw_w_key(key, part):
    spread = (1.0 / D) ** 0.5
    values = jax.random.normal(jax.random.fold_in(key, 424), (D, KVH * HD), jnp.float32) * spread
    values = jnp.clip(values, -6.0 * spread, 6.0 * spread)
    return values.astype(jnp.bfloat16)


def draw_hidden(key, part):
    values = jnp.clip(jax.random.normal(jax.random.fold_in(key, 505), (DOCUMENT_TOKENS, D), jnp.float32), -6.0, 6.0)
    return values.astype(jnp.bfloat16)


def raised(values, key, source, target, shards_of, factor):
    def block_of(position):
        return (jnp.arange(values.shape[position]) // (values.shape[position] // shards_of)).reshape((-1,) + (1,) * (values.ndim - 1 - position))

    first = jax.random.permutation(key, shards_of)[block_of(target)]
    other_side = (block_of(target) + shards_of // 2) % shards_of
    return jnp.where((block_of(source) == first) | (block_of(source) == other_side), factor * values, values)


def shard_levels(own_key, dims, shards, low, high):
    level, own = 1.0, jax.random.fold_in(own_key, 6)
    for axis_at, shards_of in shards:
        heights = jnp.exp(jax.random.uniform(jax.random.fold_in(own, axis_at), (shards_of,), jnp.float32, low / len(shards), high / len(shards)))
        level = level * jnp.repeat(heights, dims[axis_at] // shards_of).reshape([-1 if axis == axis_at else 1 for axis in range(len(dims))])
    return level


def gaussian(rng, dims, scale, bound, shards=(), held_as=jnp.bfloat16):
    result = scale * jax.random.normal(rng, dims, jnp.float32)
    if shards:
        result = result * shard_levels(rng, dims, shards, -0.22, 0.18)
    return jnp.clip(result, -bound, bound).astype(held_as)


def gaussian_with(stream_key, dims, deviation, bound, pieces, heavy, kind=jnp.bfloat16):
    values = deviation * jax.random.normal(stream_key, dims, jnp.float32)
    if pieces:
        values = values * shard_levels(stream_key, dims, pieces, -0.22, 0.18)
    return jnp.clip(raised(values, jax.random.fold_in(stream_key, 3), *heavy), -bound, bound).astype(kind)


def setup_inputs(seed: int = 0) -> dict:
    seeds = jax.random.split(jax.random.key(seed), 8)
    return {
        "hidden": draw_hidden(jax.random.fold_in(seeds[7], 71), 0),
        "depth": draw_depth(jax.random.fold_in(seeds[7], 71), 0),
        "norm_gain": draw_norm_gain(jax.random.fold_in(seeds[7], 71), 0),
        "w_query": draw_w_query(jax.random.fold_in(seeds[7], 71), 0),
        "w_key": draw_w_key(jax.random.fold_in(seeds[7], 71), 0),
        "w_value": gaussian(seeds[5], (D, KVH * HD), D ** -0.5, 0.09375, ((0, 16), (1, 2))),
        "w_out": gaussian_with(seeds[6], (QH * HD, D), (QH * HD) ** -0.5, 0.1875, ((0, 2), (1, 16)), (0, 1, 16, 2.0)),
    }


EPSILON = 1e-05
MASKED_SCORE = -1e+30

def reference(hidden, depth, norm_gain, w_query, w_key, w_value, w_out):
    blocks = DOCUMENT_TOKENS // TOK_DEV
    widened = hidden.astype(jnp.float32)
    inverse = lax.rsqrt(lax.optimization_barrier(jnp.mean(widened * widened, axis=1, keepdims=True)) + EPSILON)
    normed = (widened * inverse * norm_gain[None, :]).astype(jnp.bfloat16)
    queries = jnp.dot(normed, w_query, preferred_element_type=jnp.float32).astype(jnp.bfloat16)
    keys_all = jnp.dot(normed, w_key, preferred_element_type=jnp.float32).astype(jnp.bfloat16)
    values_all = jnp.dot(normed, w_value, preferred_element_type=jnp.float32).astype(jnp.bfloat16)
    living = (depth > STEP).reshape(blocks, TOK_DEV)
    slot_of = jnp.cumsum(living.astype(jnp.int32), axis=1) - 1
    slot_ids = jnp.arange(CAP, dtype=jnp.int32)
    hit_bool = living[:, :, None] & (slot_of[:, :, None] == slot_ids[None, None, :])
    select_tokens = hit_bool.astype(jnp.float32)

    def compact(matrix):
        shaped = matrix.astype(jnp.float32).reshape(blocks, TOK_DEV, -1)
        return jnp.einsum('src,srf->scf', select_tokens, shaped).reshape(blocks * CAP, -1)
    positions = jnp.arange(DOCUMENT_TOKENS, dtype=jnp.int32).reshape(blocks, TOK_DEV)
    slot_pos = lax.optimization_barrier(jnp.sum(jnp.where(hit_bool, positions[:, :, None], 0), axis=1))
    filled = jnp.any(hit_bool, axis=1)
    slot_pos = jnp.where(filled, slot_pos, DOCUMENT_TOKENS).reshape(blocks * CAP).astype(jnp.int32)
    group_size = QH // KVH
    kept_queries = compact(queries).reshape(blocks, CAP, QH, HD)
    kept_keys = jnp.repeat(compact(keys_all).reshape(blocks * CAP, KVH, HD), group_size, axis=1)
    kept_values = jnp.repeat(compact(values_all).reshape(blocks * CAP, KVH, HD), group_size, axis=1)
    scale = 1.0 / math.sqrt(HD)

    def attend(query_block):
        query_rows, query_pos = query_block
        scores = jnp.einsum('qhd,khd->hqk', query_rows, kept_keys) * scale
        visible = slot_pos[None, :] <= query_pos[:, None]
        scores = jnp.where(visible[None], scores, MASKED_SCORE)
        row_peak = lax.optimization_barrier(jnp.max(scores, axis=-1, keepdims=True))
        expons = jnp.exp(scores - row_peak)
        row_total = lax.optimization_barrier(jnp.sum(expons, axis=-1))
        weights = lax.optimization_barrier(expons.astype(jnp.bfloat16)).astype(jnp.float32)
        weighted = jnp.einsum('hqk,khd->qhd', weights, kept_values)
        return (weighted / jnp.transpose(row_total)[:, :, None]).astype(jnp.bfloat16)
    attended_kept = lax.map(attend, (kept_queries, slot_pos.reshape(blocks, CAP)))
    attended = jnp.einsum('src,scf->srf', select_tokens, attended_kept.reshape(blocks, CAP, QH * HD).astype(jnp.float32))
    attended = attended.reshape(DOCUMENT_TOKENS, QH * HD).astype(jnp.bfloat16)
    head_cols = QH * HD // N_TENSOR
    grouped = jnp.transpose(attended.reshape(DOCUMENT_TOKENS, N_TENSOR, head_cols), (1, 0, 2))
    out_groups = w_out.reshape(N_TENSOR, head_cols, D)

    def add_group(prefix_total, group_pair):
        columns, out_rows = group_pair
        partial_term = jnp.dot(columns, out_rows, preferred_element_type=jnp.float32)
        rounded = lax.optimization_barrier(partial_term.astype(jnp.bfloat16)).astype(jnp.float32)
        return (prefix_total + rounded, None)
    summed, _ = lax.scan(add_group, jnp.zeros((DOCUMENT_TOKENS, D), jnp.float32), (grouped, out_groups))
    living_flat = living.reshape(DOCUMENT_TOKENS)
    return jnp.where(living_flat[:, None], summed, 0.0).astype(jnp.bfloat16)
```

```python
import jax
import jax.numpy as jnp
from jax import lax
from jax.sharding import PartitionSpec as P

HD = 128
STEP = 2
EPSILON = 1e-05
MASKED_SCORE = -1e30


def rolled(pieces, axis, my):
    n = len(pieces)
    if n == 1:
        return pieces[0]
    width = pieces[0].shape[axis]
    twice = jnp.concatenate(pieces + pieces, axis=axis)
    start = lax.rem(n - my, n) * width
    return lax.dynamic_slice_in_dim(twice, start, n * width, axis=axis)


def body(n_seq, n_tensor, hidden, depth, norm_gain, w_query, w_key, w_value, w_out):
    rows, width = hidden.shape
    slots = rows // 2
    d_model = width * n_tensor
    kv_heads = w_key.shape[1] // HD
    group = w_query.shape[1] // w_key.shape[1]
    J = kv_heads
    Z = n_seq // J
    part = w_query.shape[0]
    head_cols = (group + 2) * HD
    me = lax.axis_index("seq")
    t = lax.axis_index("tensor")
    j = lax.rem(me, J)
    z = me // J
    z_groups = [[a * J + b for a in range(Z)] for b in range(J)]

    def shift_j(value, k):
        pairs = [(a * J + b, a * J + (b + k) % J) for a in range(Z) for b in range(J)]
        return lax.ppermute(value, "seq", pairs)

    def shift_t(value, k):
        return lax.ppermute(value, "tensor", [(b, (b + k) % n_tensor) for b in range(n_tensor)])

    def gather_z(value, axis):
        return lax.all_gather(value, "seq", axis=axis, tiled=True, axis_index_groups=z_groups)

    def gather_j(value):
        return [value] + [shift_j(value, J - m) for m in range(1, J)]

    def exchange_j(block_for):
        return [block_for(j)] + [
            shift_j(block_for(lax.rem(j + J - m, J)), J - m) for m in range(1, J)
        ]

    living = depth > STEP
    index = jnp.arange(rows, dtype=jnp.int32)
    rank = jnp.sum(
        jnp.where(living[None, :] & (index[None, :] <= index[:, None]), 1, 0), axis=1
    ) - 1
    slot_ids = jnp.arange(slots, dtype=jnp.int32)
    select = (living[None, :] & (rank[None, :] == slot_ids[:, None])).astype(jnp.bfloat16)
    filled = jnp.sum(select.astype(jnp.float32), axis=1).astype(jnp.bfloat16)
    packed = jnp.dot(select, hidden, preferred_element_type=jnp.float32).astype(jnp.bfloat16)

    def columns_of(i):
        return jnp.concatenate(
            [
                lax.dynamic_slice_in_dim(w_query, i * group * HD, group * HD, axis=1),
                lax.dynamic_slice_in_dim(w_key, i * HD, HD, axis=1),
                lax.dynamic_slice_in_dim(w_value, i * HD, HD, axis=1),
            ],
            axis=1,
        )

    w_rows = rolled(exchange_j(columns_of), 0, j)
    weights = gather_z(w_rows, 0)
    out_rows = group * HD
    twice = jnp.concatenate([w_out, w_out], axis=0) if J > 1 else w_out
    w_out_turned = lax.dynamic_slice_in_dim(twice, j * out_rows, J * out_rows, axis=0)
    out_weights = gather_z(w_out_turned, 1)

    features = rolled([packed] + [shift_t(packed, n_tensor - m) for m in range(1, n_tensor)], 1, t)
    widened = features.astype(jnp.float32)
    inverse = lax.rsqrt(jnp.mean(widened * widened, axis=1, keepdims=True) + EPSILON)
    normed = (widened * inverse * norm_gain[None, :]).astype(jnp.bfloat16)
    block_rows = J * slots
    tokens = jnp.concatenate(gather_j(normed), axis=0)
    flags = jnp.concatenate(gather_j(filled), axis=0)

    qkv = jnp.dot(tokens, weights, preferred_element_type=jnp.float32).astype(jnp.bfloat16)
    queries = qkv[:, : group * HD].reshape(block_rows, group, HD)
    kv = qkv[:, group * HD :]
    flag_rows = -(-block_rows // (2 * HD))
    flag_pad = -(-flag_rows // 16) * 16
    flag_block = jnp.pad(flags, (0, flag_pad * 2 * HD - block_rows)).reshape(flag_pad, 2 * HD)
    arrived = gather_z(jnp.concatenate([kv, flag_block], axis=0), 0).reshape(
        Z, block_rows + flag_pad, 2 * HD
    )
    keys = arrived[:, :block_rows, :HD].reshape(Z * block_rows, HD)
    values = arrived[:, :block_rows, HD:].reshape(Z * block_rows, HD)
    key_flags = arrived[:, block_rows:].reshape(Z, -1)[:, :block_rows].reshape(Z * block_rows)

    local = jnp.arange(block_rows, dtype=jnp.int32)
    turned = lax.rem(local // slots + j, J) * slots + lax.rem(local, slots)
    query_pos = z * block_rows + turned
    key_pos = (jnp.arange(Z, dtype=jnp.int32)[:, None] * block_rows + turned[None, :]).reshape(-1)
    visible = (key_flags[None, :] > 0) & (key_pos[None, :] <= query_pos[:, None])
    scores = jnp.einsum(
        "qgd,kd->gqk", queries, keys, preferred_element_type=jnp.float32
    ) * HD ** (-0.5)
    scores = jnp.where(visible[None], scores, MASKED_SCORE)
    expons = jnp.exp(scores - jnp.max(scores, axis=-1, keepdims=True))
    total = jnp.sum(expons, axis=-1)
    weighted = jnp.einsum(
        "gqk,kd->gqd", expons.astype(jnp.bfloat16), values, preferred_element_type=jnp.float32
    )
    attended = (weighted / total[..., None]).astype(jnp.bfloat16)
    attended = jnp.transpose(attended, (1, 0, 2)).reshape(block_rows, group * HD)
    attended = rolled([attended[m * slots : (m + 1) * slots] for m in range(J)], 0, j)

    heads = jnp.concatenate(gather_j(attended), axis=1)
    terms = jnp.dot(heads, out_weights, preferred_element_type=jnp.float32).astype(jnp.bfloat16)
    own_cols = out_weights.shape[1] // Z
    mine = exchange_j(lambda i: lax.dynamic_slice_in_dim(terms, i * slots, slots, axis=0))
    mine = [piece.reshape(slots, Z, 1, own_cols) for piece in mine]
    mine = rolled(mine, 2, j).reshape(slots, d_model)

    def features_of(i):
        return lax.dynamic_slice_in_dim(mine, i * width, width, axis=1)

    owned = features_of(t).astype(jnp.float32)
    for k in range(1, n_tensor):
        owned = owned + shift_t(features_of(lax.rem(t + k, n_tensor)), k).astype(jnp.float32)
    mixed = owned.astype(jnp.bfloat16)
    return jnp.einsum(
        "sr,sf->rf", select, mixed, preferred_element_type=jnp.float32
    ).astype(jnp.bfloat16)


def solution(mesh):
    n_seq, n_tensor = mesh.shape["seq"], mesh.shape["tensor"]

    def step(*args):
        return body(n_seq, n_tensor, *args)

    return jax.shard_map(
        step,
        mesh=mesh,
        in_specs=(
            P("seq", "tensor"),
            P("seq"),
            P(),
            P("seq", "tensor"),
            P("seq", "tensor"),
            P("seq", "tensor"),
            P("tensor", "seq"),
        ),
        out_specs=P("seq", "tensor"),
        check_vma=False,
    )
```

```python
import jax
import jax.numpy as jnp
from jax import lax
from jax.sharding import PartitionSpec as P

HD = 128
STEP = 2
EPSILON = 1e-05
MASKED_SCORE = -1e30


def rolled(pieces, axis, my):
    n = len(pieces)
    if n == 1:
        return pieces[0]
    width = pieces[0].shape[axis]
    twice = jnp.concatenate(pieces + pieces, axis=axis)
    start = lax.rem(n - my, n) * width
    return lax.dynamic_slice_in_dim(twice, start, n * width, axis=axis)


def body(n_seq, n_tensor, hidden, depth, norm_gain, w_query, w_key, w_value, w_out):
    rows, width = hidden.shape
    slots = rows // 2
    d_model = width * n_tensor
    kv_heads = w_key.shape[1] // HD
    group = w_query.shape[1] // w_key.shape[1]
    J = kv_heads
    Z = n_seq // J
    part = w_query.shape[0]
    head_cols = (group + 2) * HD
    me = lax.axis_index("seq")
    t = lax.axis_index("tensor")
    j = lax.rem(me, J)
    z = me // J
    z_groups = [[a * J + b for a in range(Z)] for b in range(J)]

    def shift_j(value, k):
        pairs = [(a * J + b, a * J + (b + k) % J) for a in range(Z) for b in range(J)]
        return lax.ppermute(value, "seq", pairs)

    def shift_t(value, k):
        return lax.ppermute(value, "tensor", [(b, (b + k) % n_tensor) for b in range(n_tensor)])

    def gather_z(value, axis):
        return lax.all_gather(value, "seq", axis=axis, tiled=True, axis_index_groups=z_groups)

    def move_z(value, k, wrap):
        pairs = [
            (a * J + b, (a + k) % Z * J + b)
            for a in range(Z)
            for b in range(J)
            if wrap or 0 <= a + k < Z
        ]
        return lax.ppermute(value, "seq", pairs)

    def chain_z(value):
        ups, downs = [], []
        up = down = value
        for _ in range(1, Z):
            up, down = move_z(up, 1, False), move_z(down, -1, False)
            ups.append(up)
            downs.append(down)
        return ups, downs

    def gather_j(value):
        return [value] + [shift_j(value, J - m) for m in range(1, J)]

    def exchange_j(block_for):
        return [block_for(j)] + [
            shift_j(block_for(lax.rem(j + J - m, J)), J - m) for m in range(1, J)
        ]

    living = depth > STEP
    index = jnp.arange(rows, dtype=jnp.int32)
    rank = jnp.sum(
        jnp.where(living[None, :] & (index[None, :] <= index[:, None]), 1, 0), axis=1
    ) - 1
    slot_ids = jnp.arange(slots, dtype=jnp.int32)
    select = (living[None, :] & (rank[None, :] == slot_ids[:, None])).astype(jnp.bfloat16)
    filled = jnp.sum(select.astype(jnp.float32), axis=1).astype(jnp.bfloat16)
    packed = jnp.dot(select, hidden, preferred_element_type=jnp.float32).astype(jnp.bfloat16)

    def columns_of(i):
        return jnp.concatenate(
            [
                lax.dynamic_slice_in_dim(w_query, i * group * HD, group * HD, axis=1),
                lax.dynamic_slice_in_dim(w_key, i * HD, HD, axis=1),
                lax.dynamic_slice_in_dim(w_value, i * HD, HD, axis=1),
            ],
            axis=1,
        )

    pieces = exchange_j(columns_of)
    out_rows = group * HD
    twice = jnp.concatenate([w_out, w_out], axis=0) if J > 1 else w_out
    w_out_turned = lax.dynamic_slice_in_dim(twice, j * out_rows, J * out_rows, axis=0)
    chained = Z <= 8

    features = rolled([packed] + [shift_t(packed, n_tensor - m) for m in range(1, n_tensor)], 1, t)
    widened = features.astype(jnp.float32)
    inverse = lax.rsqrt(jnp.mean(widened * widened, axis=1, keepdims=True) + EPSILON)
    normed = (widened * inverse * norm_gain[None, :]).astype(jnp.bfloat16)
    block_rows = J * slots
    tokens = jnp.concatenate(gather_j(normed), axis=0)
    flags = jnp.concatenate(gather_j(filled), axis=0)

    if chained:
        cuts = [pieces[:1], pieces[1:2], pieces[2:]] if J > 2 else [pieces[:1], pieces[1:]]
        cuts = [jnp.concatenate(cut, axis=0) for cut in cuts if cut]
        chains = [chain_z(cut) for cut in cuts]
        shaped = tokens.reshape(block_rows, Z, J, part)
        if J > 1:
            shaped = lax.dynamic_slice_in_dim(
                jnp.concatenate([shaped, shaped], axis=2), j, J, axis=2
            )
        turned_tokens = shaped.reshape(block_rows, d_model)

        def product(matrix, source, offset):
            start = jnp.clip(source, 0, Z - 1) * (J * part) + offset
            return jnp.dot(
                lax.dynamic_slice_in_dim(turned_tokens, start, matrix.shape[0], axis=1),
                matrix,
                preferred_element_type=jnp.float32,
            )

        offset, qkv_sum = 0, None
        for cut, (ups, downs) in zip(cuts, chains):
            terms = [product(cut, z, offset)]
            for k in range(1, Z):
                terms.append(product(ups[k - 1], z - k, offset))
                terms.append(product(downs[k - 1], z + k, offset))
            for term in terms:
                qkv_sum = term if qkv_sum is None else qkv_sum + term
            offset += cut.shape[0]
        qkv = qkv_sum.astype(jnp.bfloat16)
    else:
        weights = gather_z(rolled(pieces, 0, j), 0)
        qkv = jnp.dot(tokens, weights, preferred_element_type=jnp.float32).astype(jnp.bfloat16)
    queries = qkv[:, : group * HD].reshape(block_rows, group, HD)
    kv = qkv[:, group * HD :]
    flag_rows = -(-block_rows // (2 * HD))
    flag_pad = -(-flag_rows // 16) * 16
    flag_block = jnp.pad(flags, (0, flag_pad * 2 * HD - block_rows)).reshape(flag_pad, 2 * HD)
    parcel = jnp.concatenate([kv, flag_block], axis=0)
    if chained:
        arrived = jnp.stack([parcel] + [move_z(parcel, Z - m, True) for m in range(1, Z)])
        sources = lax.rem(jnp.arange(Z, dtype=jnp.int32) + z, Z)
    else:
        arrived = gather_z(parcel, 0).reshape(Z, block_rows + flag_pad, 2 * HD)
        sources = jnp.arange(Z, dtype=jnp.int32)
    keys = arrived[:, :block_rows, :HD].reshape(Z * block_rows, HD)
    values = arrived[:, :block_rows, HD:].reshape(Z * block_rows, HD)
    key_flags = arrived[:, block_rows:].reshape(Z, -1)[:, :block_rows].reshape(Z * block_rows)

    local = jnp.arange(block_rows, dtype=jnp.int32)
    turned = lax.rem(local // slots + j, J) * slots + lax.rem(local, slots)
    query_pos = z * block_rows + turned
    key_pos = (sources[:, None] * block_rows + turned[None, :]).reshape(-1)
    visible = (key_flags[None, :] > 0) & (key_pos[None, :] <= query_pos[:, None])
    scores = jnp.einsum(
        "qgd,kd->gqk", queries, keys, preferred_element_type=jnp.float32
    ) * HD ** (-0.5)
    scores = jnp.where(visible[None], scores, MASKED_SCORE)
    expons = jnp.exp(scores - jnp.max(scores, axis=-1, keepdims=True))
    total = jnp.sum(expons, axis=-1)
    weighted = jnp.einsum(
        "gqk,kd->gqd", expons.astype(jnp.bfloat16), values, preferred_element_type=jnp.float32
    )
    attended = (weighted / total[..., None]).astype(jnp.bfloat16)
    attended = jnp.transpose(attended, (1, 0, 2)).reshape(block_rows, group * HD)
    attended = rolled([attended[m * slots : (m + 1) * slots] for m in range(J)], 0, j)

    heads = jnp.concatenate(gather_j(attended), axis=1)
    if chained:
        w_first = lax.optimization_barrier((w_out_turned, qkv[:1]))[0] if Z > 1 else w_out_turned
        up1, down1 = move_z(w_first, 1, False), move_z(w_first, -1, False)
        ups, downs = [up1], [down1]
        up, down, _ = lax.optimization_barrier((up1, down1, arrived[:, :1]))
        for _ in range(2, Z):
            up, down = move_z(up, 1, False), move_z(down, -1, False)
            ups.append(up)
            downs.append(down)

        def projected(matrix):
            return jnp.dot(heads, matrix, preferred_element_type=jnp.float32).astype(jnp.bfloat16)

        columns = [projected(w_out_turned)]
        for m in range(1, Z):
            columns.append(
                jnp.where(z + m < Z, projected(downs[m - 1]), projected(ups[Z - m - 1]))
            )
        terms = rolled(columns, 1, z)
    else:
        out_weights = gather_z(w_out_turned, 1)
        terms = jnp.dot(heads, out_weights, preferred_element_type=jnp.float32).astype(jnp.bfloat16)
    own_cols = w_out.shape[1]
    mine = exchange_j(lambda i: lax.dynamic_slice_in_dim(terms, i * slots, slots, axis=0))
    mine = [piece.reshape(slots, Z, 1, own_cols) for piece in mine]
    mine = rolled(mine, 2, j).reshape(slots, d_model)

    def features_of(i):
        return lax.dynamic_slice_in_dim(mine, i * width, width, axis=1)

    owned = features_of(t).astype(jnp.float32)
    for k in range(1, n_tensor):
        owned = owned + shift_t(features_of(lax.rem(t + k, n_tensor)), k).astype(jnp.float32)
    mixed = owned.astype(jnp.bfloat16)
    return jnp.einsum(
        "sr,sf->rf", select, mixed, preferred_element_type=jnp.float32
    ).astype(jnp.bfloat16)


def solution(mesh):
    n_seq, n_tensor = mesh.shape["seq"], mesh.shape["tensor"]

    def step(*args):
        return body(n_seq, n_tensor, *args)

    return jax.shard_map(
        step,
        mesh=mesh,
        in_specs=(
            P("seq", "tensor"),
            P("seq"),
            P(),
            P("seq", "tensor"),
            P("seq", "tensor"),
            P("seq", "tensor"),
            P("tensor", "seq"),
        ),
        out_specs=P("seq", "tensor"),
        check_vma=False,
    )
```

```python
import functools

import jax
import jax.numpy as jnp
from jax import lax
from jax.experimental import pallas as pl
from jax.experimental.pallas import tpu as pltpu
from jax.sharding import PartitionSpec as P

HD = 128
STEP = 2
EPSILON = 1e-05
MASKED_SCORE = -1e30


def rolled(pieces, axis, my):
    n = len(pieces)
    if n == 1:
        return pieces[0]
    width = pieces[0].shape[axis]
    twice = jnp.concatenate(pieces + pieces, axis=axis)
    start = lax.rem(n - my, n) * width
    return lax.dynamic_slice_in_dim(twice, start, n * width, axis=axis)


PAD = 16
MESH = pl.DeviceIdType.MESH


def gather_kernel(
    J, Z, T, packed, flags, gain, w_blocks, w_out, q_ref, kv_ref, outw_ref,
    features, tokens, weights, total,
    xs, _xr, fs, fr, ts, tr, ws_up, ws_dn, wr, ks_up, ks_dn, kr, os_up, os_dn, orr,
):
    me, t = lax.axis_index("seq"), lax.axis_index("tensor")
    z, j = me // J, lax.rem(me, J)
    slots, width = packed.shape
    block = slots + PAD
    rows = J * block
    part, cols = w_blocks.shape[1:]
    q_cols = q_ref.shape[1]

    def peer_j(m):
        return (z * J + lax.rem(j + m, J), t)

    def peer_t(m):
        return (me, lax.rem(t + m, T))

    up, down = (me + J, t), (me - J, t)
    has_up, has_down = z < Z - 1, z > 0

    barrier = pltpu.get_barrier_semaphore()
    for m in range(1, J):
        pl.semaphore_signal(barrier, inc=1, device_id=peer_j(m), device_id_type=MESH)
    for m in range(1, T):
        pl.semaphore_signal(barrier, inc=1, device_id=peer_t(m), device_id_type=MESH)

    @pl.when(has_up)
    def _():
        pl.semaphore_signal(barrier, inc=1, device_id=up, device_id_type=MESH)

    @pl.when(has_down)
    def _():
        pl.semaphore_signal(barrier, inc=1, device_id=down, device_id_type=MESH)

    pl.semaphore_wait(
        barrier, J + T - 2 + has_up.astype(jnp.int32) + has_down.astype(jnp.int32)
    )

    def send(src, dst, send_sem, recv_sem, device):
        return pltpu.make_async_remote_copy(
            src_ref=src, dst_ref=dst, send_sem=send_sem, recv_sem=recv_sem,
            device_id=device, device_id_type=MESH,
        )

    def w_at(zb, jb):
        return weights.at[pl.ds(pl.multiple_of((zb * J + jb) * part, part), part), :]

    def w_exchange(m):
        return send(w_blocks.at[lax.rem(j + m, J)], w_at(z, j), xs.at[m], wr.at[z * J + j], peer_j(m))

    def w_copy(zb, jb, sems, device, own=False):
        src = w_blocks.at[j] if own else w_at(zb, jb)
        return send(src, w_at(zb, jb), sems.at[zb * J + jb], wr.at[zb * J + jb], device)

    def f_copy(m):
        return send(packed, features.at[t], fs.at[m], fr.at[t], peer_t(m))

    def t_at(jb):
        return tokens.at[pl.ds(pl.multiple_of(jb * block, block), block), :]

    def t_copy(m):
        return send(t_at(j), t_at(j), ts.at[m], tr.at[j], peer_j(m))

    def both(start_up, start_down):
        pl.when(has_up)(start_up)
        pl.when(has_down)(start_down)

    def push_w(zb, jb, own=False):
        both(
            lambda: w_copy(zb, jb, ws_up, up, own).start(),
            lambda: w_copy(zb, jb, ws_dn, down, own).start(),
        )

    for m in range(1, T):
        f_copy(m).start()
    for m in range(1, J):
        w_exchange(m).start()
    push_w(z, j, own=True)
    weights[pl.ds(pl.multiple_of(me * part, part), part), :] = w_blocks[j]
    features[t] = packed[...]
    for m in range(1, T):
        tb = lax.rem(t + m, T)
        send(packed, features.at[tb], fs.at[m], fr.at[tb], peer_t(m)).wait_recv()

    squares = jnp.zeros((slots, 1), jnp.float32)
    for tb in range(T):
        wide = features[tb].astype(jnp.float32)
        squares += jnp.sum(wide * wide, axis=1, keepdims=True)
    inverse = lax.rsqrt(squares / (T * width) + EPSILON)
    own_row = pl.multiple_of(j * block, block)
    for tb in range(T):
        at = slice(tb * width, (tb + 1) * width)
        wide = features[tb].astype(jnp.float32) * inverse * gain[:, at]
        tokens[pl.ds(own_row, slots), at] = wide.astype(jnp.bfloat16)
    tokens[pl.ds(pl.multiple_of(own_row + slots, PAD), PAD), :] = flags[...]
    for m in range(1, J):
        t_copy(m).start()

    for m in range(1, J):
        jb = lax.rem(j + m, J)
        w_copy(z, jb, ws_up, up).wait_recv()
        push_w(z, jb)
    for m in range(1, J):
        jb = lax.rem(j + m, J)
        send(t_at(jb), t_at(jb), ts.at[m], tr.at[jb], peer_j(m)).wait_recv()

    depth = J * part

    def product(zb):
        at = pl.ds(pl.multiple_of(zb * depth, depth), depth)
        return jnp.dot(tokens[:, at], weights[at, :], preferred_element_type=jnp.float32)

    total[...] = product(z)
    for k in range(1, Z):
        for m in range(J):
            jb = lax.rem(j + m, J)

            @pl.when(z - k >= 0)
            def _():
                w_copy(z - k, jb, ws_up, up).wait_recv()

                @pl.when(has_up)
                def _():
                    w_copy(z - k, jb, ws_up, up).start()

            @pl.when(z + k < Z)
            def _():
                w_copy(z + k, jb, ws_dn, down).wait_recv()

                @pl.when(has_down)
                def _():
                    w_copy(z + k, jb, ws_dn, down).start()

        @pl.when(z - k >= 0)
        def _():
            total[...] += product(z - k)

        @pl.when(z + k < Z)
        def _():
            total[...] += product(z + k)

    q_ref[...] = total[:, :q_cols].astype(jnp.bfloat16)

    def k_at(zb):
        return kv_ref.at[pl.ds(pl.multiple_of(zb * rows, rows), rows), :]

    kv_row = pl.multiple_of(z * rows, rows)
    kv_ref[pl.ds(kv_row, rows), :] = total[:, q_cols:].astype(jnp.bfloat16)
    for jb in range(J):
        kv_ref[pl.ds(pl.multiple_of(kv_row + jb * block + slots, PAD), PAD), :] = tokens[
            jb * block + slots : (jb + 1) * block, : cols - q_cols
        ]

    def k_copy(zb, sems, device):
        return send(k_at(zb), k_at(zb), sems.at[zb], kr.at[zb], device)

    def o_copy(zb, sems, device, own=False):
        src = w_out if own else outw_ref.at[zb]
        return send(src, outw_ref.at[zb], sems.at[zb], orr.at[zb], device)

    both(lambda: k_copy(z, ks_up, up).start(), lambda: k_copy(z, ks_dn, down).start())
    both(
        lambda: o_copy(z, os_up, up, True).start(), lambda: o_copy(z, os_dn, down, True).start()
    )
    outw_ref[z] = w_out[...]
    for copy, up_sems, dn_sems in ((k_copy, ks_up, ks_dn), (o_copy, os_up, os_dn)):
        for k in range(1, Z):

            @pl.when(z - k >= 0)
            def _():
                copy(z - k, up_sems, up).wait_recv()

                @pl.when(has_up)
                def _():
                    copy(z - k, up_sems, up).start()

            @pl.when(z + k < Z)
            def _():
                copy(z + k, dn_sems, down).wait_recv()

                @pl.when(has_down)
                def _():
                    copy(z + k, dn_sems, down).start()

    for m in range(1, T):
        f_copy(m).wait_send()
    for m in range(1, J):
        w_exchange(m).wait_send()
        t_copy(m).wait_send()
    for zb in range(Z):
        for up_way, sems_of, device in ((True, (ws_up, ks_up, os_up), up), (False, (ws_dn, ks_dn, os_dn), down)):
            sent = has_up & (zb <= z) if up_way else has_down & (zb >= z)

            @pl.when(sent)
            def _():
                for jb in range(J):
                    w_copy(zb, jb, sems_of[0], device).wait_send()
                k_copy(zb, sems_of[1], device).wait_send()
                o_copy(zb, sems_of[2], device).wait_send()


def gathered(J, Z, T, packed, flags, gain, w_blocks, w_out):
    slots, width = packed.shape
    part, cols = w_blocks.shape[1:]
    rows = J * (slots + PAD)
    q_cols = cols - 2 * HD
    vmem = pl.BlockSpec(memory_space=pltpu.VMEM)
    dma = pltpu.SemaphoreType.DMA
    return pl.pallas_call(
        functools.partial(gather_kernel, J, Z, T),
        out_shape=(
            jax.ShapeDtypeStruct((rows, q_cols), jnp.bfloat16),
            jax.ShapeDtypeStruct((Z * rows, 2 * HD), jnp.bfloat16),
            jax.ShapeDtypeStruct((Z,) + w_out.shape, jnp.bfloat16),
        ),
        in_specs=[vmem] * 5,
        out_specs=(vmem,) * 3,
        scratch_shapes=[
            pltpu.VMEM((T, slots, width), jnp.bfloat16),
            pltpu.VMEM((rows, T * width), jnp.bfloat16),
            pltpu.VMEM((T * width, cols), jnp.bfloat16),
            pltpu.VMEM((rows, cols), jnp.float32),
            dma((J,)), dma((J,)), dma((T,)), dma((T,)), dma((J,)), dma((J,)),
            dma((Z * J,)), dma((Z * J,)), dma((Z * J,)),
            dma((Z,)), dma((Z,)), dma((Z,)), dma((Z,)), dma((Z,)), dma((Z,)),
        ],
        compiler_params=pltpu.CompilerParams(
            collective_id=0, has_side_effects=True, vmem_limit_bytes=48 * 1024 * 1024
        ),
    )(packed, flags, gain, w_blocks, w_out)


def body(n_seq, n_tensor, hidden, depth, norm_gain, w_query, w_key, w_value, w_out):
    rows, width = hidden.shape
    slots = rows // 2
    d_model = width * n_tensor
    kv_heads = w_key.shape[1] // HD
    group = w_query.shape[1] // w_key.shape[1]
    J = kv_heads
    Z = n_seq // J
    part = w_query.shape[0]
    head_cols = (group + 2) * HD
    me = lax.axis_index("seq")
    t = lax.axis_index("tensor")
    j = lax.rem(me, J)
    z = me // J
    z_groups = [[a * J + b for a in range(Z)] for b in range(J)]

    def shift_j(value, k):
        pairs = [(a * J + b, a * J + (b + k) % J) for a in range(Z) for b in range(J)]
        return lax.ppermute(value, "seq", pairs)

    def shift_t(value, k):
        return lax.ppermute(value, "tensor", [(b, (b + k) % n_tensor) for b in range(n_tensor)])

    def gather_z(value, axis):
        return lax.all_gather(value, "seq", axis=axis, tiled=True, axis_index_groups=z_groups)

    def gather_j(value):
        return [value] + [shift_j(value, J - m) for m in range(1, J)]

    def exchange_j(block_for):
        return [block_for(j)] + [
            shift_j(block_for(lax.rem(j + J - m, J)), J - m) for m in range(1, J)
        ]

    living = depth > STEP
    index = jnp.arange(rows, dtype=jnp.int32)
    rank = jnp.sum(
        jnp.where(living[None, :] & (index[None, :] <= index[:, None]), 1, 0), axis=1
    ) - 1
    slot_ids = jnp.arange(slots, dtype=jnp.int32)
    select = (living[None, :] & (rank[None, :] == slot_ids[:, None])).astype(jnp.bfloat16)
    filled = jnp.sum(select.astype(jnp.float32), axis=1).astype(jnp.bfloat16)
    packed = jnp.dot(select, hidden, preferred_element_type=jnp.float32).astype(jnp.bfloat16)

    def columns_of(i):
        return jnp.concatenate(
            [
                lax.dynamic_slice_in_dim(w_query, i * group * HD, group * HD, axis=1),
                lax.dynamic_slice_in_dim(w_key, i * HD, HD, axis=1),
                lax.dynamic_slice_in_dim(w_value, i * HD, HD, axis=1),
            ],
            axis=1,
        )

    fast = 1 < Z <= 8 and J > 1 and n_tensor > 1 and slots % 16 == 0 and slots <= 128
    fast = fast and w_out.shape[1] % 128 == 0 and part % 16 == 0
    if fast:
        flag_rows = jnp.broadcast_to(
            jnp.pad(filled, (0, d_model - slots))[None, :], (PAD, d_model)
        )
        w_blocks = jnp.stack([columns_of(i) for i in range(J)])
        queries, arrived, out_weights = gathered(
            J, Z, n_tensor, packed, flag_rows, norm_gain[None, :], w_blocks, w_out
        )
        block_rows = queries.shape[0]
        queries = queries.reshape(block_rows, group, HD)
        keys, values = arrived[:, :HD], arrived[:, HD:]
        marks = arrived.reshape(n_seq, slots + PAD, 2 * HD)[:, slots, : slots + PAD]
        key_flags = marks.reshape(n_seq * (slots + PAD))
        key_pos = jnp.arange(n_seq * (slots + PAD), dtype=jnp.int32)
        query_pos = z * block_rows + jnp.arange(block_rows, dtype=jnp.int32)
        visible = (key_flags[None, :] > 0) & (key_pos[None, :] <= query_pos[:, None])
    else:
        w_rows = rolled(exchange_j(columns_of), 0, j)
        weights = gather_z(w_rows, 0)
        out_rows = group * HD
        twice = jnp.concatenate([w_out, w_out], axis=0) if J > 1 else w_out
        w_out_turned = lax.dynamic_slice_in_dim(twice, j * out_rows, J * out_rows, axis=0)
        out_weights = gather_z(w_out_turned, 1)

        features = rolled([packed] + [shift_t(packed, n_tensor - m) for m in range(1, n_tensor)], 1, t)
        widened = features.astype(jnp.float32)
        inverse = lax.rsqrt(jnp.mean(widened * widened, axis=1, keepdims=True) + EPSILON)
        normed = (widened * inverse * norm_gain[None, :]).astype(jnp.bfloat16)
        block_rows = J * slots
        tokens = jnp.concatenate(gather_j(normed), axis=0)
        flags = jnp.concatenate(gather_j(filled), axis=0)

        qkv = jnp.dot(tokens, weights, preferred_element_type=jnp.float32).astype(jnp.bfloat16)
        queries = qkv[:, : group * HD].reshape(block_rows, group, HD)
        kv = qkv[:, group * HD :]
        flag_rows = -(-block_rows // (2 * HD))
        flag_pad = -(-flag_rows // 16) * 16
        flag_block = jnp.pad(flags, (0, flag_pad * 2 * HD - block_rows)).reshape(flag_pad, 2 * HD)
        arrived = gather_z(jnp.concatenate([kv, flag_block], axis=0), 0).reshape(
            Z, block_rows + flag_pad, 2 * HD
        )
        keys = arrived[:, :block_rows, :HD].reshape(Z * block_rows, HD)
        values = arrived[:, :block_rows, HD:].reshape(Z * block_rows, HD)
        key_flags = arrived[:, block_rows:].reshape(Z, -1)[:, :block_rows].reshape(Z * block_rows)

        local = jnp.arange(block_rows, dtype=jnp.int32)
        turned = lax.rem(local // slots + j, J) * slots + lax.rem(local, slots)
        query_pos = z * block_rows + turned
        key_pos = (jnp.arange(Z, dtype=jnp.int32)[:, None] * block_rows + turned[None, :]).reshape(-1)
        visible = (key_flags[None, :] > 0) & (key_pos[None, :] <= query_pos[:, None])
    scores = jnp.einsum(
        "qgd,kd->gqk", queries, keys, preferred_element_type=jnp.float32
    ) * HD ** (-0.5)
    scores = jnp.where(visible[None], scores, MASKED_SCORE)
    expons = jnp.exp(scores - jnp.max(scores, axis=-1, keepdims=True))
    total = jnp.sum(expons, axis=-1)
    weighted = jnp.einsum(
        "gqk,kd->gqd", expons.astype(jnp.bfloat16), values, preferred_element_type=jnp.float32
    )
    attended = (weighted / total[..., None]).astype(jnp.bfloat16)
    attended = jnp.transpose(attended, (1, 0, 2)).reshape(block_rows, group * HD)
    if fast:
        attended = attended.reshape(J, slots + PAD, group * HD)[:, :slots]
        attended = attended.reshape(J * slots, group * HD)
        heads = rolled(gather_j(attended), 1, j)
        terms = jnp.concatenate(
            [
                jnp.dot(heads, out_weights[a], preferred_element_type=jnp.float32)
                for a in range(Z)
            ],
            axis=1,
        ).astype(jnp.bfloat16)
    else:
        attended = rolled([attended[m * slots : (m + 1) * slots] for m in range(J)], 0, j)
        heads = jnp.concatenate(gather_j(attended), axis=1)
        terms = jnp.dot(heads, out_weights, preferred_element_type=jnp.float32).astype(jnp.bfloat16)
    own_cols = w_out.shape[1]
    mine = exchange_j(lambda i: lax.dynamic_slice_in_dim(terms, i * slots, slots, axis=0))
    mine = [piece.reshape(slots, Z, 1, own_cols) for piece in mine]
    mine = rolled(mine, 2, j).reshape(slots, d_model)

    def features_of(i):
        return lax.dynamic_slice_in_dim(mine, i * width, width, axis=1)

    owned = features_of(t).astype(jnp.float32)
    for k in range(1, n_tensor):
        owned = owned + shift_t(features_of(lax.rem(t + k, n_tensor)), k).astype(jnp.float32)
    mixed = owned.astype(jnp.bfloat16)
    return jnp.einsum(
        "sr,sf->rf", select, mixed, preferred_element_type=jnp.float32
    ).astype(jnp.bfloat16)


def solution(mesh):
    n_seq, n_tensor = mesh.shape["seq"], mesh.shape["tensor"]

    def step(*args):
        return body(n_seq, n_tensor, *args)

    return jax.shard_map(
        step,
        mesh=mesh,
        in_specs=(
            P("seq", "tensor"),
            P("seq"),
            P(),
            P("seq", "tensor"),
            P("seq", "tensor"),
            P("seq", "tensor"),
            P("tensor", "seq"),
        ),
        out_specs=P("seq", "tensor"),
        check_vma=False,
    )
```

```python
import functools

import jax
import jax.numpy as jnp
from jax import lax
from jax.experimental import pallas as pl
from jax.experimental.pallas import tpu as pltpu
from jax.sharding import PartitionSpec as P

HD = 128
STEP = 2
EPSILON = 1e-05
MASKED_SCORE = -1e30


def rolled(pieces, axis, my):
    n = len(pieces)
    if n == 1:
        return pieces[0]
    width = pieces[0].shape[axis]
    twice = jnp.concatenate(pieces + pieces, axis=axis)
    start = lax.rem(n - my, n) * width
    return lax.dynamic_slice_in_dim(twice, start, n * width, axis=axis)


LANES = 128
MESH = pl.DeviceIdType.MESH


def gather_kernel(
    J, Z, T, packed, flags, gain, w_blocks, w_out, mixed_ref,
    q_ref, kv_ref, outw_ref, features, tokens, weights, total, seen, heads, terms, mine, other,
    xs, _xr, fs, fr, ts, tr, ws_up, ws_dn, wr, ks_up, ks_dn, kr, os_up, os_dn, orr,
    hs, hr, ms, mr, ys, yr,
):
    me, t = lax.axis_index("seq"), lax.axis_index("tensor")
    z, j = me // J, lax.rem(me, J)
    slots, width = packed.shape
    block = LANES
    PAD = block - slots
    rows = J * block
    part, cols = w_blocks.shape[1:]
    q_cols = q_ref.shape[1]

    def peer_j(m):
        return (z * J + lax.rem(j + m, J), t)

    def peer_t(m):
        return (me, lax.rem(t + m, T))

    up, down = (me + J, t), (me - J, t)
    has_up, has_down = z < Z - 1, z > 0

    barrier = pltpu.get_barrier_semaphore()
    for m in range(1, J):
        pl.semaphore_signal(barrier, inc=1, device_id=peer_j(m), device_id_type=MESH)
    for m in range(1, T):
        pl.semaphore_signal(barrier, inc=1, device_id=peer_t(m), device_id_type=MESH)

    @pl.when(has_up)
    def _():
        pl.semaphore_signal(barrier, inc=1, device_id=up, device_id_type=MESH)

    @pl.when(has_down)
    def _():
        pl.semaphore_signal(barrier, inc=1, device_id=down, device_id_type=MESH)

    pl.semaphore_wait(
        barrier, J + T - 2 + has_up.astype(jnp.int32) + has_down.astype(jnp.int32)
    )

    def send(src, dst, send_sem, recv_sem, device):
        return pltpu.make_async_remote_copy(
            src_ref=src, dst_ref=dst, send_sem=send_sem, recv_sem=recv_sem,
            device_id=device, device_id_type=MESH,
        )

    def w_at(zb, jb):
        return weights.at[pl.ds(pl.multiple_of((zb * J + jb) * part, part), part), :]

    def w_exchange(m):
        return send(w_blocks.at[lax.rem(j + m, J)], w_at(z, j), xs.at[m], wr.at[z * J + j], peer_j(m))

    def w_copy(zb, jb, sems, device, own=False):
        src = w_blocks.at[j] if own else w_at(zb, jb)
        return send(src, w_at(zb, jb), sems.at[zb * J + jb], wr.at[zb * J + jb], device)

    def f_copy(m):
        return send(packed, features.at[t], fs.at[m], fr.at[t], peer_t(m))

    def t_at(jb):
        return tokens.at[pl.ds(pl.multiple_of(jb * block, block), block), :]

    def t_copy(m):
        return send(t_at(j), t_at(j), ts.at[m], tr.at[j], peer_j(m))

    def both(start_up, start_down):
        pl.when(has_up)(start_up)
        pl.when(has_down)(start_down)

    def push_w(zb, jb, own=False):
        both(
            lambda: w_copy(zb, jb, ws_up, up, own).start(),
            lambda: w_copy(zb, jb, ws_dn, down, own).start(),
        )

    for m in range(1, T):
        f_copy(m).start()
    for m in range(1, J):
        w_exchange(m).start()
    push_w(z, j, own=True)
    weights[pl.ds(pl.multiple_of(me * part, part), part), :] = w_blocks[j]
    features[t] = packed[...]
    for m in range(1, T):
        tb = lax.rem(t + m, T)
        send(packed, features.at[tb], fs.at[m], fr.at[tb], peer_t(m)).wait_recv()

    squares = jnp.zeros((slots, 1), jnp.float32)
    for tb in range(T):
        wide = features[tb].astype(jnp.float32)
        squares += jnp.sum(wide * wide, axis=1, keepdims=True)
    inverse = lax.rsqrt(squares / (T * width) + EPSILON)
    own_row = pl.multiple_of(j * block, block)
    for tb in range(T):
        at = slice(tb * width, (tb + 1) * width)
        wide = features[tb].astype(jnp.float32) * inverse * gain[:, at]
        tokens[pl.ds(own_row, slots), at] = wide.astype(jnp.bfloat16)
    tokens[pl.ds(pl.multiple_of(own_row + slots, 16), PAD), :] = flags[...]
    for m in range(1, J):
        t_copy(m).start()

    for m in range(1, J):
        jb = lax.rem(j + m, J)
        w_copy(z, jb, ws_up, up).wait_recv()
        push_w(z, jb)
    for m in range(1, J):
        jb = lax.rem(j + m, J)
        send(t_at(jb), t_at(jb), ts.at[m], tr.at[jb], peer_j(m)).wait_recv()

    depth = J * part

    def product(zb):
        at = pl.ds(pl.multiple_of(zb * depth, depth), depth)
        return jnp.dot(tokens[:, at], weights[at, :], preferred_element_type=jnp.float32)

    total[...] = product(z)
    for k in range(1, Z):
        for m in range(J):
            jb = lax.rem(j + m, J)

            @pl.when(z - k >= 0)
            def _():
                w_copy(z - k, jb, ws_up, up).wait_recv()

                @pl.when(has_up)
                def _():
                    w_copy(z - k, jb, ws_up, up).start()

            @pl.when(z + k < Z)
            def _():
                w_copy(z + k, jb, ws_dn, down).wait_recv()

                @pl.when(has_down)
                def _():
                    w_copy(z + k, jb, ws_dn, down).start()

        @pl.when(z - k >= 0)
        def _():
            total[...] += product(z - k)

        @pl.when(z + k < Z)
        def _():
            total[...] += product(z + k)

    q_ref[...] = total[:, :q_cols].astype(jnp.bfloat16)

    def k_at(zb):
        return kv_ref.at[pl.ds(pl.multiple_of(zb * rows, rows), rows), :]

    kv_row = pl.multiple_of(z * rows, rows)
    kv_ref[pl.ds(kv_row, rows), :] = total[:, q_cols:].astype(jnp.bfloat16)
    for jb in range(J):
        kv_ref[pl.ds(pl.multiple_of(kv_row + jb * block + slots, 16), PAD), :] = tokens[
            jb * block + slots : (jb + 1) * block, : cols - q_cols
        ]

    def k_copy(zb, sems, device):
        return send(k_at(zb), k_at(zb), sems.at[zb], kr.at[zb], device)

    def o_copy(zb, sems, device, own=False):
        src = w_out if own else outw_ref.at[zb]
        return send(src, outw_ref.at[zb], sems.at[zb], orr.at[zb], device)

    def relay(copy, k, up_sems, dn_sems):
        @pl.when(z - k >= 0)
        def _():
            copy(z - k, up_sems, up).wait_recv()

            @pl.when(has_up)
            def _():
                copy(z - k, up_sems, up).start()

        @pl.when(z + k < Z)
        def _():
            copy(z + k, dn_sems, down).wait_recv()

            @pl.when(has_down)
            def _():
                copy(z + k, dn_sems, down).start()

    both(lambda: k_copy(z, ks_up, up).start(), lambda: k_copy(z, ks_dn, down).start())
    for k in range(1, Z):
        if k == Z - 1:
            both(
                lambda: o_copy(z, os_up, up, True).start(),
                lambda: o_copy(z, os_dn, down, True).start(),
            )
        relay(k_copy, k, ks_up, ks_dn)
    outw_ref[z] = w_out[...]

    for b in range(Z * J):
        seen[:, b * block : (b + 1) * block] = kv_ref[
            b * block + slots : b * block + slots + 16, :block
        ].astype(jnp.float32)
    key_pos = lax.broadcasted_iota(jnp.int32, (slots, Z * rows), 1)
    row_pos = lax.broadcasted_iota(jnp.int32, (slots, Z * rows), 0)

    @pl.loop(0, J)
    def _(jb):
        top = pl.multiple_of(jb * block, block)
        out_top = pl.multiple_of(jb * slots, 16)
        visible = (seen[0:1, :] > 0) & (key_pos <= row_pos + z * rows + top)
        for g in range(q_cols // HD):
            at = slice(g * HD, (g + 1) * HD)
            scores = lax.dot_general(
                q_ref[pl.ds(top, slots), at],
                kv_ref[:, :HD],
                (((1,), (1,)), ((), ())),
                preferred_element_type=jnp.float32,
            ) * HD ** (-0.5)
            scores = jnp.where(visible, scores, MASKED_SCORE)
            expons = jnp.exp(scores - jnp.max(scores, axis=1, keepdims=True))
            row_total = jnp.sum(expons, axis=1, keepdims=True)
            weighted = jnp.dot(
                expons.astype(jnp.bfloat16), kv_ref[:, HD:], preferred_element_type=jnp.float32
            )
            heads[j, pl.ds(out_top, slots), at] = (weighted / row_total).astype(jnp.bfloat16)

    def h_copy(m):
        return send(heads.at[j], heads.at[j], hs.at[m], hr.at[j], peer_j(m))

    for m in range(1, J):
        h_copy(m).start()
    relay(o_copy, 1, os_up, os_dn)
    for m in range(1, J):
        jb = lax.rem(j + m, J)
        send(heads.at[jb], heads.at[jb], hs.at[m], hr.at[jb], peer_j(m)).wait_recv()

    def m_copy(zb, m):
        to = lax.rem(j + m, J)
        return send(
            terms.at[zb * J + to], mine.at[zb * J + j], ms.at[zb * J + m], mr.at[zb * J + j], peer_j(m)
        )

    def emit(zb):
        result = None
        for jb in range(J):
            term = jnp.dot(
                heads[jb],
                outw_ref[zb, jb * q_cols : (jb + 1) * q_cols, :],
                preferred_element_type=jnp.float32,
            )
            result = term if result is None else result + term
        rounded = result.astype(jnp.bfloat16)
        for jb in range(J):
            terms[zb * J + jb] = rounded[jb * slots : (jb + 1) * slots]
        for m in range(1, J):
            m_copy(zb, m).start()
        mine[zb * J + j] = terms[zb * J + j]

    share = Z // T

    def y_copy(zb):
        to = zb // share
        return send(
            mine.at[pl.ds(zb * J, J)],
            other.at[t, pl.ds(lax.rem(zb, share) * J, J)],
            ys.at[zb],
            yr.at[t * share + lax.rem(zb, share)],
            (me, to),
        )

    def collect(zb):
        for m in range(1, J):
            jb = lax.rem(j + m, J)
            send(
                terms.at[zb * J + jb], mine.at[zb * J + jb], ms.at[zb * J + m], mr.at[zb * J + jb], peer_j(m)
            ).wait_recv()

        @pl.when(zb // share != t)
        def _():
            y_copy(zb).start()

    def steps(k, act):
        if k == 0:
            act(z)
        else:
            pl.when(z - k >= 0)(lambda: act(z - k))
            pl.when(z + k < Z)(lambda: act(z + k))

    steps(0, emit)
    for k in range(1, Z):
        if k > 1:
            relay(o_copy, k, os_up, os_dn)
        steps(k, emit)
        steps(k - 1, collect)
    steps(Z - 1, collect)

    for m in range(1, T):
        tb = lax.rem(t + m, T)
        for zl in range(share):
            at = pl.ds(zl * J, J)
            send(
                mine.at[at], other.at[tb, at], ys.at[zl], yr.at[tb * share + zl], peer_t(m)
            ).wait_recv()
    for b in range(share * J):
        owned = mine[t * share * J + b].astype(jnp.float32)
        for m in range(1, T):
            owned += other[lax.rem(t + m, T), b].astype(jnp.float32)
        mixed_ref[:, b * part : (b + 1) * part] = owned.astype(jnp.bfloat16)

    for m in range(1, T):
        f_copy(m).wait_send()
    for m in range(1, J):
        w_exchange(m).wait_send()
        t_copy(m).wait_send()
        h_copy(m).wait_send()
    for zb in range(Z):
        for m in range(1, J):
            m_copy(zb, m).wait_send()

        @pl.when(zb // share != t)
        def _():
            y_copy(zb).wait_send()

        for up_way, sems_of, device in ((True, (ws_up, ks_up, os_up), up), (False, (ws_dn, ks_dn, os_dn), down)):
            sent = has_up & (zb <= z) if up_way else has_down & (zb >= z)

            @pl.when(sent)
            def _():
                for jb in range(J):
                    w_copy(zb, jb, sems_of[0], device).wait_send()
                k_copy(zb, sems_of[1], device).wait_send()
                o_copy(zb, sems_of[2], device).wait_send()


def gathered(J, Z, T, packed, flags, gain, w_blocks, w_out):
    slots, width = packed.shape
    part, cols = w_blocks.shape[1:]
    rows = J * LANES
    q_cols = cols - 2 * HD
    vmem = pl.BlockSpec(memory_space=pltpu.VMEM)
    dma = pltpu.SemaphoreType.DMA
    bf16 = jnp.bfloat16
    return pl.pallas_call(
        functools.partial(gather_kernel, J, Z, T),
        out_shape=jax.ShapeDtypeStruct((slots, width), bf16),
        in_specs=[vmem] * 5,
        out_specs=vmem,
        scratch_shapes=[
            pltpu.VMEM((rows, q_cols), bf16),
            pltpu.VMEM((Z * rows, 2 * HD), bf16),
            pltpu.VMEM((Z,) + w_out.shape, bf16),
            pltpu.VMEM((T, slots, width), bf16),
            pltpu.VMEM((rows, T * width), bf16),
            pltpu.VMEM((T * width, cols), bf16),
            pltpu.VMEM((rows, cols), jnp.float32),
            pltpu.VMEM((16, Z * rows), jnp.float32),
            pltpu.VMEM((J, J * slots, q_cols), bf16),
            pltpu.VMEM((Z * J, slots, w_out.shape[1]), bf16),
            pltpu.VMEM((Z * J, slots, w_out.shape[1]), bf16),
            pltpu.VMEM((T, Z // T * J, slots, w_out.shape[1]), bf16),
            dma((J,)), dma((J,)), dma((T,)), dma((T,)), dma((J,)), dma((J,)),
            dma((Z * J,)), dma((Z * J,)), dma((Z * J,)),
            dma((Z,)), dma((Z,)), dma((Z,)), dma((Z,)), dma((Z,)), dma((Z,)),
            dma((J,)), dma((J,)), dma((Z * J,)), dma((Z * J,)), dma((Z,)), dma((Z,)),
        ],
        compiler_params=pltpu.CompilerParams(
            collective_id=0, has_side_effects=True, vmem_limit_bytes=48 * 1024 * 1024
        ),
    )(packed, flags, gain, w_blocks, w_out)


def body(n_seq, n_tensor, hidden, depth, norm_gain, w_query, w_key, w_value, w_out):
    rows, width = hidden.shape
    slots = rows // 2
    d_model = width * n_tensor
    kv_heads = w_key.shape[1] // HD
    group = w_query.shape[1] // w_key.shape[1]
    J = kv_heads
    Z = n_seq // J
    part = w_query.shape[0]
    head_cols = (group + 2) * HD
    me = lax.axis_index("seq")
    t = lax.axis_index("tensor")
    j = lax.rem(me, J)
    z = me // J
    z_groups = [[a * J + b for a in range(Z)] for b in range(J)]

    def shift_j(value, k):
        pairs = [(a * J + b, a * J + (b + k) % J) for a in range(Z) for b in range(J)]
        return lax.ppermute(value, "seq", pairs)

    def shift_t(value, k):
        return lax.ppermute(value, "tensor", [(b, (b + k) % n_tensor) for b in range(n_tensor)])

    def gather_z(value, axis):
        return lax.all_gather(value, "seq", axis=axis, tiled=True, axis_index_groups=z_groups)

    def gather_j(value):
        return [value] + [shift_j(value, J - m) for m in range(1, J)]

    def exchange_j(block_for):
        return [block_for(j)] + [
            shift_j(block_for(lax.rem(j + J - m, J)), J - m) for m in range(1, J)
        ]

    living = depth > STEP
    index = jnp.arange(rows, dtype=jnp.int32)
    rank = jnp.sum(
        jnp.where(living[None, :] & (index[None, :] <= index[:, None]), 1, 0), axis=1
    ) - 1
    slot_ids = jnp.arange(slots, dtype=jnp.int32)
    select = (living[None, :] & (rank[None, :] == slot_ids[:, None])).astype(jnp.bfloat16)
    filled = jnp.sum(select.astype(jnp.float32), axis=1).astype(jnp.bfloat16)
    packed = jnp.dot(select, hidden, preferred_element_type=jnp.float32).astype(jnp.bfloat16)

    def columns_of(i):
        return jnp.concatenate(
            [
                lax.dynamic_slice_in_dim(w_query, i * group * HD, group * HD, axis=1),
                lax.dynamic_slice_in_dim(w_key, i * HD, HD, axis=1),
                lax.dynamic_slice_in_dim(w_value, i * HD, HD, axis=1),
            ],
            axis=1,
        )

    fast = 1 < Z <= 8 and J > 1 and n_tensor > 1 and slots % 16 == 0 and slots <= LANES - 16 and Z % n_tensor == 0 and part == w_out.shape[1]
    fast = fast and w_out.shape[1] % 128 == 0 and part % 16 == 0
    if fast:
        flag_rows = jnp.broadcast_to(
            jnp.pad(filled, (0, d_model - slots))[None, :], (LANES - slots, d_model)
        )
        w_blocks = jnp.stack([columns_of(i) for i in range(J)])
        mixed = gathered(J, Z, n_tensor, packed, flag_rows, norm_gain[None, :], w_blocks, w_out)
        return jnp.einsum(
            "sr,sf->rf", select, mixed, preferred_element_type=jnp.float32
        ).astype(jnp.bfloat16)

    w_rows = rolled(exchange_j(columns_of), 0, j)
    weights = gather_z(w_rows, 0)
    out_rows = group * HD
    twice = jnp.concatenate([w_out, w_out], axis=0) if J > 1 else w_out
    w_out_turned = lax.dynamic_slice_in_dim(twice, j * out_rows, J * out_rows, axis=0)
    out_weights = gather_z(w_out_turned, 1)

    features = rolled([packed] + [shift_t(packed, n_tensor - m) for m in range(1, n_tensor)], 1, t)
    widened = features.astype(jnp.float32)
    inverse = lax.rsqrt(jnp.mean(widened * widened, axis=1, keepdims=True) + EPSILON)
    normed = (widened * inverse * norm_gain[None, :]).astype(jnp.bfloat16)
    block_rows = J * slots
    tokens = jnp.concatenate(gather_j(normed), axis=0)
    flags = jnp.concatenate(gather_j(filled), axis=0)

    qkv = jnp.dot(tokens, weights, preferred_element_type=jnp.float32).astype(jnp.bfloat16)
    queries = qkv[:, : group * HD].reshape(block_rows, group, HD)
    kv = qkv[:, group * HD :]
    flag_rows = -(-block_rows // (2 * HD))
    flag_pad = -(-flag_rows // 16) * 16
    flag_block = jnp.pad(flags, (0, flag_pad * 2 * HD - block_rows)).reshape(flag_pad, 2 * HD)
    arrived = gather_z(jnp.concatenate([kv, flag_block], axis=0), 0).reshape(
        Z, block_rows + flag_pad, 2 * HD
    )
    keys = arrived[:, :block_rows, :HD].reshape(Z * block_rows, HD)
    values = arrived[:, :block_rows, HD:].reshape(Z * block_rows, HD)
    key_flags = arrived[:, block_rows:].reshape(Z, -1)[:, :block_rows].reshape(Z * block_rows)

    local = jnp.arange(block_rows, dtype=jnp.int32)
    turned = lax.rem(local // slots + j, J) * slots + lax.rem(local, slots)
    query_pos = z * block_rows + turned
    key_pos = (jnp.arange(Z, dtype=jnp.int32)[:, None] * block_rows + turned[None, :]).reshape(-1)
    visible = (key_flags[None, :] > 0) & (key_pos[None, :] <= query_pos[:, None])
    scores = jnp.einsum(
        "qgd,kd->gqk", queries, keys, preferred_element_type=jnp.float32
    ) * HD ** (-0.5)
    scores = jnp.where(visible[None], scores, MASKED_SCORE)
    expons = jnp.exp(scores - jnp.max(scores, axis=-1, keepdims=True))
    total = jnp.sum(expons, axis=-1)
    weighted = jnp.einsum(
        "gqk,kd->gqd", expons.astype(jnp.bfloat16), values, preferred_element_type=jnp.float32
    )
    attended = (weighted / total[..., None]).astype(jnp.bfloat16)
    attended = jnp.transpose(attended, (1, 0, 2)).reshape(block_rows, group * HD)
    attended = rolled([attended[m * slots : (m + 1) * slots] for m in range(J)], 0, j)
    heads = jnp.concatenate(gather_j(attended), axis=1)
    terms = jnp.dot(heads, out_weights, preferred_element_type=jnp.float32).astype(jnp.bfloat16)
    own_cols = w_out.shape[1]
    mine = exchange_j(lambda i: lax.dynamic_slice_in_dim(terms, i * slots, slots, axis=0))
    mine = [piece.reshape(slots, Z, 1, own_cols) for piece in mine]
    mine = rolled(mine, 2, j).reshape(slots, d_model)

    def features_of(i):
        return lax.dynamic_slice_in_dim(mine, i * width, width, axis=1)

    owned = features_of(t).astype(jnp.float32)
    for k in range(1, n_tensor):
        owned = owned + shift_t(features_of(lax.rem(t + k, n_tensor)), k).astype(jnp.float32)
    mixed = owned.astype(jnp.bfloat16)
    return jnp.einsum(
        "sr,sf->rf", select, mixed, preferred_element_type=jnp.float32
    ).astype(jnp.bfloat16)


def solution(mesh):
    n_seq, n_tensor = mesh.shape["seq"], mesh.shape["tensor"]

    def step(*args):
        return body(n_seq, n_tensor, *args)

    return jax.shard_map(
        step,
        mesh=mesh,
        in_specs=(
            P("seq", "tensor"),
            P("seq"),
            P(),
            P("seq", "tensor"),
            P("seq", "tensor"),
            P("seq", "tensor"),
            P("tensor", "seq"),
        ),
        out_specs=P("seq", "tensor"),
        check_vma=False,
    )
```

```python
import functools

import jax
import jax.numpy as jnp
from jax import lax
from jax.experimental import pallas as pl
from jax.experimental.pallas import tpu as pltpu
from jax.sharding import PartitionSpec as P

HD = 128
STEP = 2
EPSILON = 1e-05
MASKED_SCORE = -1e30


def rolled(pieces, axis, my):
    n = len(pieces)
    if n == 1:
        return pieces[0]
    width = pieces[0].shape[axis]
    twice = jnp.concatenate(pieces + pieces, axis=axis)
    start = lax.rem(n - my, n) * width
    return lax.dynamic_slice_in_dim(twice, start, n * width, axis=axis)


LANES = 128
MESH = pl.DeviceIdType.MESH


def gather_kernel(
    J, Z, T, packed, flags, gain, w_blocks, w_out, mixed_ref,
    q_ref, kv_ref, outw_ref, features, tokens, weights, total, seen, heads, terms, mine, other,
    xs, _xr, fs, fr, ts, tr, ws_up, ws_dn, wr, ks_up, ks_dn, kr, os_up, os_dn, orr,
    hs, hr, ms, mr, ys, yr,
):
    me, t = lax.axis_index("seq"), lax.axis_index("tensor")
    z, j = me // J, lax.rem(me, J)
    slots, width = packed.shape
    block = LANES
    PAD = block - slots
    rows = J * block
    part, cols = w_blocks.shape[1:]
    q_cols = q_ref.shape[1]

    def peer_j(m):
        return (z * J + lax.rem(j + m, J), t)

    def peer_t(m):
        return (me, lax.rem(t + m, T))

    up, down = (me + J, t), (me - J, t)
    has_up, has_down = z < Z - 1, z > 0

    barrier = pltpu.get_barrier_semaphore()
    for m in range(1, J):
        pl.semaphore_signal(barrier, inc=1, device_id=peer_j(m), device_id_type=MESH)
    for m in range(1, T):
        pl.semaphore_signal(barrier, inc=1, device_id=peer_t(m), device_id_type=MESH)

    @pl.when(has_up)
    def _():
        pl.semaphore_signal(barrier, inc=1, device_id=up, device_id_type=MESH)

    @pl.when(has_down)
    def _():
        pl.semaphore_signal(barrier, inc=1, device_id=down, device_id_type=MESH)

    pl.semaphore_wait(
        barrier, J + T - 2 + has_up.astype(jnp.int32) + has_down.astype(jnp.int32)
    )

    def send(src, dst, send_sem, recv_sem, device):
        return pltpu.make_async_remote_copy(
            src_ref=src, dst_ref=dst, send_sem=send_sem, recv_sem=recv_sem,
            device_id=device, device_id_type=MESH,
        )

    def w_at(zb, jb):
        return weights.at[pl.ds(pl.multiple_of((zb * J + jb) * part, part), part), :]

    def w_exchange(m):
        return send(w_blocks.at[lax.rem(j + m, J)], w_at(z, j), xs.at[m], wr.at[z * J + j], peer_j(m))

    def w_copy(zb, jb, sems, device, own=False):
        src = w_blocks.at[j] if own else w_at(zb, jb)
        return send(src, w_at(zb, jb), sems.at[zb * J + jb], wr.at[zb * J + jb], device)

    def f_copy(m):
        return send(packed, features.at[t], fs.at[m], fr.at[t], peer_t(m))

    def t_at(jb):
        return tokens.at[pl.ds(pl.multiple_of(jb * block, block), slots + 16), :]

    def t_copy(m):
        return send(t_at(j), t_at(j), ts.at[m], tr.at[j], peer_j(m))

    def both(start_up, start_down):
        pl.when(has_up)(start_up)
        pl.when(has_down)(start_down)

    def push_w(zb, jb, own=False):
        both(
            lambda: w_copy(zb, jb, ws_up, up, own).start(),
            lambda: w_copy(zb, jb, ws_dn, down, own).start(),
        )

    for m in range(1, T):
        f_copy(m).start()
    for m in range(1, J):
        w_exchange(m).start()
    push_w(z, j, own=True)
    weights[pl.ds(pl.multiple_of(me * part, part), part), :] = w_blocks[j]
    features[t] = packed[...]
    for m in range(1, T):
        tb = lax.rem(t + m, T)
        send(packed, features.at[tb], fs.at[m], fr.at[tb], peer_t(m)).wait_recv()

    squares = jnp.zeros((slots, 1), jnp.float32)
    for tb in range(T):
        wide = features[tb].astype(jnp.float32)
        squares += jnp.sum(wide * wide, axis=1, keepdims=True)
    inverse = lax.rsqrt(squares / (T * width) + EPSILON)
    own_row = pl.multiple_of(j * block, block)
    for tb in range(T):
        at = slice(tb * width, (tb + 1) * width)
        wide = features[tb].astype(jnp.float32) * inverse * gain[:, at]
        tokens[pl.ds(own_row, slots), at] = wide.astype(jnp.bfloat16)
    tokens[pl.ds(pl.multiple_of(own_row + slots, 16), 16), :] = flags[...]
    for jb in range(J):
        tokens[jb * block + slots + 16 : (jb + 1) * block, :] = jnp.zeros(
            (PAD - 16, T * width), jnp.bfloat16
        )
    for m in range(1, J):
        t_copy(m).start()

    for m in range(1, J):
        jb = lax.rem(j + m, J)
        w_copy(z, jb, ws_up, up).wait_recv()
        push_w(z, jb)
    depth = J * part

    def product(zb):
        at = pl.ds(pl.multiple_of(zb * depth, depth), depth)
        return jnp.dot(tokens[:, at], weights[at, :], preferred_element_type=jnp.float32)

    def add_products(k):
        @pl.when(z - k >= 0)
        def _():
            total[...] += product(z - k)

        @pl.when(z + k < Z)
        def _():
            total[...] += product(z + k)

    for k in range(1, Z):
        if k == Z - 1:
            for m in range(1, J):
                jb = lax.rem(j + m, J)
                send(t_at(jb), t_at(jb), ts.at[m], tr.at[jb], peer_j(m)).wait_recv()
            total[...] = product(z)
            for done in range(1, k):
                add_products(done)
        for m in range(J):
            jb = lax.rem(j + m, J)

            @pl.when(z - k >= 0)
            def _():
                w_copy(z - k, jb, ws_up, up).wait_recv()

                @pl.when(has_up)
                def _():
                    w_copy(z - k, jb, ws_up, up).start()

            @pl.when(z + k < Z)
            def _():
                w_copy(z + k, jb, ws_dn, down).wait_recv()

                @pl.when(has_down)
                def _():
                    w_copy(z + k, jb, ws_dn, down).start()

    add_products(Z - 1)

    q_ref[...] = total[:, :q_cols].astype(jnp.bfloat16)

    def k_at(zb):
        return kv_ref.at[pl.ds(pl.multiple_of(zb * rows, rows), rows), :]

    kv_row = pl.multiple_of(z * rows, rows)
    kv_ref[pl.ds(kv_row, rows), :] = total[:, q_cols:].astype(jnp.bfloat16)
    for jb in range(J):
        kv_ref[pl.ds(pl.multiple_of(kv_row + jb * block + slots, 16), PAD), :] = tokens[
            jb * block + slots : (jb + 1) * block, : cols - q_cols
        ]

    def k_copy(zb, sems, device):
        return send(k_at(zb), k_at(zb), sems.at[zb], kr.at[zb], device)

    def o_copy(zb, sems, device, own=False):
        src = w_out if own else outw_ref.at[zb]
        return send(src, outw_ref.at[zb], sems.at[zb], orr.at[zb], device)

    def relay(copy, k, up_sems, dn_sems):
        @pl.when(z - k >= 0)
        def _():
            copy(z - k, up_sems, up).wait_recv()

            @pl.when(has_up)
            def _():
                copy(z - k, up_sems, up).start()

        @pl.when(z + k < Z)
        def _():
            copy(z + k, dn_sems, down).wait_recv()

            @pl.when(has_down)
            def _():
                copy(z + k, dn_sems, down).start()

    both(lambda: k_copy(z, ks_up, up).start(), lambda: k_copy(z, ks_dn, down).start())
    for k in range(1, Z):
        if k == Z - 1:
            both(
                lambda: o_copy(z, os_up, up, True).start(),
                lambda: o_copy(z, os_dn, down, True).start(),
            )
        relay(k_copy, k, ks_up, ks_dn)
    outw_ref[z] = w_out[...]

    for b in range(Z * J):
        seen[:, b * block : (b + 1) * block] = kv_ref[
            b * block + slots : b * block + slots + 16, :block
        ].astype(jnp.float32)
    key_pos = lax.broadcasted_iota(jnp.int32, (slots, Z * rows), 1)
    row_pos = lax.broadcasted_iota(jnp.int32, (slots, Z * rows), 0)

    @pl.loop(0, J)
    def _(jb):
        top = pl.multiple_of(jb * block, block)
        out_top = pl.multiple_of(jb * slots, 16)
        visible = (seen[0:1, :] > 0) & (key_pos <= row_pos + z * rows + top)
        for g in range(q_cols // HD):
            at = slice(g * HD, (g + 1) * HD)
            scores = lax.dot_general(
                q_ref[pl.ds(top, slots), at],
                kv_ref[:, :HD],
                (((1,), (1,)), ((), ())),
                preferred_element_type=jnp.float32,
            ) * HD ** (-0.5)
            scores = jnp.where(visible, scores, MASKED_SCORE)
            expons = jnp.exp(scores - jnp.max(scores, axis=1, keepdims=True))
            row_total = jnp.sum(expons, axis=1, keepdims=True)
            weighted = jnp.dot(
                expons.astype(jnp.bfloat16), kv_ref[:, HD:], preferred_element_type=jnp.float32
            )
            heads[j, pl.ds(out_top, slots), at] = (weighted / row_total).astype(jnp.bfloat16)

    def h_copy(m):
        return send(heads.at[j], heads.at[j], hs.at[m], hr.at[j], peer_j(m))

    for m in range(1, J):
        h_copy(m).start()
    relay(o_copy, 1, os_up, os_dn)
    for m in range(1, J):
        jb = lax.rem(j + m, J)
        send(heads.at[jb], heads.at[jb], hs.at[m], hr.at[jb], peer_j(m)).wait_recv()

    def m_copy(zb, m):
        to = lax.rem(j + m, J)
        return send(
            terms.at[zb * J + to], mine.at[zb * J + j], ms.at[zb * J + m], mr.at[zb * J + j], peer_j(m)
        )

    def emit(zb):
        result = None
        for jb in range(J):
            term = jnp.dot(
                heads[jb],
                outw_ref[zb, jb * q_cols : (jb + 1) * q_cols, :],
                preferred_element_type=jnp.float32,
            )
            result = term if result is None else result + term
        rounded = result.astype(jnp.bfloat16)
        for jb in range(J):
            terms[zb * J + jb] = rounded[jb * slots : (jb + 1) * slots]
        for m in range(1, J):
            m_copy(zb, m).start()
        mine[zb * J + j] = terms[zb * J + j]

    share = Z // T

    def y_copy(zb):
        to = zb // share
        return send(
            mine.at[pl.ds(zb * J, J)],
            other.at[t, pl.ds(lax.rem(zb, share) * J, J)],
            ys.at[zb],
            yr.at[t * share + lax.rem(zb, share)],
            (me, to),
        )

    def collect(zb):
        for m in range(1, J):
            jb = lax.rem(j + m, J)
            send(
                terms.at[zb * J + jb], mine.at[zb * J + jb], ms.at[zb * J + m], mr.at[zb * J + jb], peer_j(m)
            ).wait_recv()

        @pl.when(zb // share != t)
        def _():
            y_copy(zb).start()

    def steps(k, act):
        if k == 0:
            act(z)
        else:
            pl.when(z - k >= 0)(lambda: act(z - k))
            pl.when(z + k < Z)(lambda: act(z + k))

    steps(0, emit)
    for k in range(1, Z):
        if k > 1:
            relay(o_copy, k, os_up, os_dn)
        steps(k, emit)
        steps(k - 1, collect)
    steps(Z - 1, collect)

    for m in range(1, T):
        tb = lax.rem(t + m, T)
        for zl in range(share):
            at = pl.ds(zl * J, J)
            send(
                mine.at[at], other.at[tb, at], ys.at[zl], yr.at[tb * share + zl], peer_t(m)
            ).wait_recv()
    for b in range(share * J):
        owned = mine[t * share * J + b].astype(jnp.float32)
        for m in range(1, T):
            owned += other[lax.rem(t + m, T), b].astype(jnp.float32)
        mixed_ref[:, b * part : (b + 1) * part] = owned.astype(jnp.bfloat16)

    for m in range(1, T):
        f_copy(m).wait_send()
    for m in range(1, J):
        w_exchange(m).wait_send()
        t_copy(m).wait_send()
        h_copy(m).wait_send()
    for zb in range(Z):
        for m in range(1, J):
            m_copy(zb, m).wait_send()

        @pl.when(zb // share != t)
        def _():
            y_copy(zb).wait_send()

        for up_way, sems_of, device in ((True, (ws_up, ks_up, os_up), up), (False, (ws_dn, ks_dn, os_dn), down)):
            sent = has_up & (zb <= z) if up_way else has_down & (zb >= z)

            @pl.when(sent)
            def _():
                for jb in range(J):
                    w_copy(zb, jb, sems_of[0], device).wait_send()
                k_copy(zb, sems_of[1], device).wait_send()
                o_copy(zb, sems_of[2], device).wait_send()


def gathered(J, Z, T, packed, flags, gain, w_blocks, w_out):
    slots, width = packed.shape
    part, cols = w_blocks.shape[1:]
    rows = J * LANES
    q_cols = cols - 2 * HD
    vmem = pl.BlockSpec(memory_space=pltpu.VMEM)
    dma = pltpu.SemaphoreType.DMA
    bf16 = jnp.bfloat16
    return pl.pallas_call(
        functools.partial(gather_kernel, J, Z, T),
        out_shape=jax.ShapeDtypeStruct((slots, width), bf16),
        in_specs=[vmem] * 5,
        out_specs=vmem,
        scratch_shapes=[
            pltpu.VMEM((rows, q_cols), bf16),
            pltpu.VMEM((Z * rows, 2 * HD), bf16),
            pltpu.VMEM((Z,) + w_out.shape, bf16),
            pltpu.VMEM((T, slots, width), bf16),
            pltpu.VMEM((rows, T * width), bf16),
            pltpu.VMEM((T * width, cols), bf16),
            pltpu.VMEM((rows, cols), jnp.float32),
            pltpu.VMEM((16, Z * rows), jnp.float32),
            pltpu.VMEM((J, J * slots, q_cols), bf16),
            pltpu.VMEM((Z * J, slots, w_out.shape[1]), bf16),
            pltpu.VMEM((Z * J, slots, w_out.shape[1]), bf16),
            pltpu.VMEM((T, Z // T * J, slots, w_out.shape[1]), bf16),
            dma((J,)), dma((J,)), dma((T,)), dma((T,)), dma((J,)), dma((J,)),
            dma((Z * J,)), dma((Z * J,)), dma((Z * J,)),
            dma((Z,)), dma((Z,)), dma((Z,)), dma((Z,)), dma((Z,)), dma((Z,)),
            dma((J,)), dma((J,)), dma((Z * J,)), dma((Z * J,)), dma((Z,)), dma((Z,)),
        ],
        compiler_params=pltpu.CompilerParams(
            collective_id=0, has_side_effects=True, vmem_limit_bytes=48 * 1024 * 1024
        ),
    )(packed, flags, gain, w_blocks, w_out)


def body(n_seq, n_tensor, hidden, depth, norm_gain, w_query, w_key, w_value, w_out):
    rows, width = hidden.shape
    slots = rows // 2
    d_model = width * n_tensor
    kv_heads = w_key.shape[1] // HD
    group = w_query.shape[1] // w_key.shape[1]
    J = kv_heads
    Z = n_seq // J
    part = w_query.shape[0]
    head_cols = (group + 2) * HD
    me = lax.axis_index("seq")
    t = lax.axis_index("tensor")
    j = lax.rem(me, J)
    z = me // J
    z_groups = [[a * J + b for a in range(Z)] for b in range(J)]

    def shift_j(value, k):
        pairs = [(a * J + b, a * J + (b + k) % J) for a in range(Z) for b in range(J)]
        return lax.ppermute(value, "seq", pairs)

    def shift_t(value, k):
        return lax.ppermute(value, "tensor", [(b, (b + k) % n_tensor) for b in range(n_tensor)])

    def gather_z(value, axis):
        return lax.all_gather(value, "seq", axis=axis, tiled=True, axis_index_groups=z_groups)

    def gather_j(value):
        return [value] + [shift_j(value, J - m) for m in range(1, J)]

    def exchange_j(block_for):
        return [block_for(j)] + [
            shift_j(block_for(lax.rem(j + J - m, J)), J - m) for m in range(1, J)
        ]

    living = depth > STEP
    index = jnp.arange(rows, dtype=jnp.int32)
    rank = jnp.sum(
        jnp.where(living[None, :] & (index[None, :] <= index[:, None]), 1, 0), axis=1
    ) - 1
    slot_ids = jnp.arange(slots, dtype=jnp.int32)
    select = (living[None, :] & (rank[None, :] == slot_ids[:, None])).astype(jnp.bfloat16)
    filled = jnp.sum(select.astype(jnp.float32), axis=1).astype(jnp.bfloat16)
    packed = jnp.dot(select, hidden, preferred_element_type=jnp.float32).astype(jnp.bfloat16)

    def columns_of(i):
        return jnp.concatenate(
            [
                lax.dynamic_slice_in_dim(w_query, i * group * HD, group * HD, axis=1),
                lax.dynamic_slice_in_dim(w_key, i * HD, HD, axis=1),
                lax.dynamic_slice_in_dim(w_value, i * HD, HD, axis=1),
            ],
            axis=1,
        )

    fast = 1 < Z <= 8 and J > 1 and n_tensor > 1 and slots % 16 == 0 and slots < LANES - 16 and Z % n_tensor == 0 and part == w_out.shape[1]
    fast = fast and w_out.shape[1] % 128 == 0 and part % 16 == 0
    if fast:
        flag_rows = jnp.broadcast_to(
            jnp.pad(filled, (0, d_model - slots))[None, :], (16, d_model)
        )
        w_blocks = jnp.stack([columns_of(i) for i in range(J)])
        mixed = gathered(J, Z, n_tensor, packed, flag_rows, norm_gain[None, :], w_blocks, w_out)
        return jnp.einsum(
            "sr,sf->rf", select, mixed, preferred_element_type=jnp.float32
        ).astype(jnp.bfloat16)

    w_rows = rolled(exchange_j(columns_of), 0, j)
    weights = gather_z(w_rows, 0)
    out_rows = group * HD
    twice = jnp.concatenate([w_out, w_out], axis=0) if J > 1 else w_out
    w_out_turned = lax.dynamic_slice_in_dim(twice, j * out_rows, J * out_rows, axis=0)
    out_weights = gather_z(w_out_turned, 1)

    features = rolled([packed] + [shift_t(packed, n_tensor - m) for m in range(1, n_tensor)], 1, t)
    widened = features.astype(jnp.float32)
    inverse = lax.rsqrt(jnp.mean(widened * widened, axis=1, keepdims=True) + EPSILON)
    normed = (widened * inverse * norm_gain[None, :]).astype(jnp.bfloat16)
    block_rows = J * slots
    tokens = jnp.concatenate(gather_j(normed), axis=0)
    flags = jnp.concatenate(gather_j(filled), axis=0)

    qkv = jnp.dot(tokens, weights, preferred_element_type=jnp.float32).astype(jnp.bfloat16)
    queries = qkv[:, : group * HD].reshape(block_rows, group, HD)
    kv = qkv[:, group * HD :]
    flag_rows = -(-block_rows // (2 * HD))
    flag_pad = -(-flag_rows // 16) * 16
    flag_block = jnp.pad(flags, (0, flag_pad * 2 * HD - block_rows)).reshape(flag_pad, 2 * HD)
    arrived = gather_z(jnp.concatenate([kv, flag_block], axis=0), 0).reshape(
        Z, block_rows + flag_pad, 2 * HD
    )
    keys = arrived[:, :block_rows, :HD].reshape(Z * block_rows, HD)
    values = arrived[:, :block_rows, HD:].reshape(Z * block_rows, HD)
    key_flags = arrived[:, block_rows:].reshape(Z, -1)[:, :block_rows].reshape(Z * block_rows)

    local = jnp.arange(block_rows, dtype=jnp.int32)
    turned = lax.rem(local // slots + j, J) * slots + lax.rem(local, slots)
    query_pos = z * block_rows + turned
    key_pos = (jnp.arange(Z, dtype=jnp.int32)[:, None] * block_rows + turned[None, :]).reshape(-1)
    visible = (key_flags[None, :] > 0) & (key_pos[None, :] <= query_pos[:, None])
    scores = jnp.einsum(
        "qgd,kd->gqk", queries, keys, preferred_element_type=jnp.float32
    ) * HD ** (-0.5)
    scores = jnp.where(visible[None], scores, MASKED_SCORE)
    expons = jnp.exp(scores - jnp.max(scores, axis=-1, keepdims=True))
    total = jnp.sum(expons, axis=-1)
    weighted = jnp.einsum(
        "gqk,kd->gqd", expons.astype(jnp.bfloat16), values, preferred_element_type=jnp.float32
    )
    attended = (weighted / total[..., None]).astype(jnp.bfloat16)
    attended = jnp.transpose(attended, (1, 0, 2)).reshape(block_rows, group * HD)
    attended = rolled([attended[m * slots : (m + 1) * slots] for m in range(J)], 0, j)
    heads = jnp.concatenate(gather_j(attended), axis=1)
    terms = jnp.dot(heads, out_weights, preferred_element_type=jnp.float32).astype(jnp.bfloat16)
    own_cols = w_out.shape[1]
    mine = exchange_j(lambda i: lax.dynamic_slice_in_dim(terms, i * slots, slots, axis=0))
    mine = [piece.reshape(slots, Z, 1, own_cols) for piece in mine]
    mine = rolled(mine, 2, j).reshape(slots, d_model)

    def features_of(i):
        return lax.dynamic_slice_in_dim(mine, i * width, width, axis=1)

    owned = features_of(t).astype(jnp.float32)
    for k in range(1, n_tensor):
        owned = owned + shift_t(features_of(lax.rem(t + k, n_tensor)), k).astype(jnp.float32)
    mixed = owned.astype(jnp.bfloat16)
    return jnp.einsum(
        "sr,sf->rf", select, mixed, preferred_element_type=jnp.float32
    ).astype(jnp.bfloat16)


def solution(mesh):
    n_seq, n_tensor = mesh.shape["seq"], mesh.shape["tensor"]

    def step(*args):
        return body(n_seq, n_tensor, *args)

    return jax.shard_map(
        step,
        mesh=mesh,
        in_specs=(
            P("seq", "tensor"),
            P("seq"),
            P(),
            P("seq", "tensor"),
            P("seq", "tensor"),
            P("seq", "tensor"),
            P("tensor", "seq"),
        ),
        out_specs=P("seq", "tensor"),
        check_vma=False,
    )
```

```python
import functools

import jax
import jax.numpy as jnp
from jax import lax
from jax.experimental import pallas as pl
from jax.experimental.pallas import tpu as pltpu
from jax.sharding import PartitionSpec as P

HD = 128
STEP = 2
EPSILON = 1e-05
MASKED_SCORE = -1e30


def rolled(pieces, axis, my):
    n = len(pieces)
    if n == 1:
        return pieces[0]
    width = pieces[0].shape[axis]
    twice = jnp.concatenate(pieces + pieces, axis=axis)
    start = lax.rem(n - my, n) * width
    return lax.dynamic_slice_in_dim(twice, start, n * width, axis=axis)


LANES = 128
MESH = pl.DeviceIdType.MESH


def gather_kernel(
    J, Z, T, packed, flags, gain, w_blocks, w_out, mixed_ref,
    q_ref, kv_ref, outw_ref, features, tokens, weights, total, seen, heads, terms, mine, other,
    xs, _xr, fs, fr, ts, tr, ws_up, ws_dn, wr, ks_up, ks_dn, kr, os_up, os_dn, orr,
    hs, hr, ms, mr, ys, yr,
):
    me, t = lax.axis_index("seq"), lax.axis_index("tensor")
    z, j = me // J, lax.rem(me, J)
    slots, width = packed.shape
    block = LANES
    PAD = block - slots
    rows = J * block
    part, cols = w_blocks.shape[1:]
    q_cols = q_ref.shape[1]

    def peer_j(m):
        return (z * J + lax.rem(j + m, J), t)

    def peer_t(m):
        return (me, lax.rem(t + m, T))

    up, down = (me + J, t), (me - J, t)
    has_up, has_down = z < Z - 1, z > 0

    barrier = pltpu.get_barrier_semaphore()
    for m in range(1, J):
        pl.semaphore_signal(barrier, inc=1, device_id=peer_j(m), device_id_type=MESH)
    for m in range(1, T):
        pl.semaphore_signal(barrier, inc=1, device_id=peer_t(m), device_id_type=MESH)

    @pl.when(has_up)
    def _():
        pl.semaphore_signal(barrier, inc=1, device_id=up, device_id_type=MESH)

    @pl.when(has_down)
    def _():
        pl.semaphore_signal(barrier, inc=1, device_id=down, device_id_type=MESH)

    pl.semaphore_wait(
        barrier, J + T - 2 + has_up.astype(jnp.int32) + has_down.astype(jnp.int32)
    )

    def send(src, dst, send_sem, recv_sem, device):
        return pltpu.make_async_remote_copy(
            src_ref=src, dst_ref=dst, send_sem=send_sem, recv_sem=recv_sem,
            device_id=device, device_id_type=MESH,
        )

    def w_at(zb, jb):
        return weights.at[pl.ds(pl.multiple_of((zb * J + jb) * part, part), part), :]

    def w_exchange(m):
        return send(w_blocks.at[lax.rem(j + m, J)], w_at(z, j), xs.at[m], wr.at[z * J + j], peer_j(m))

    def w_copy(zb, jb, sems, device, own=False):
        src = w_blocks.at[j] if own else w_at(zb, jb)
        return send(src, w_at(zb, jb), sems.at[zb * J + jb], wr.at[zb * J + jb], device)

    def f_copy(m):
        return send(packed, features.at[t], fs.at[m], fr.at[t], peer_t(m))

    def t_at(jb):
        return tokens.at[pl.ds(pl.multiple_of(jb * block, block), slots + 16), :]

    def t_copy(m):
        return send(t_at(j), t_at(j), ts.at[m], tr.at[j], peer_j(m))

    def both(start_up, start_down):
        pl.when(has_up)(start_up)
        pl.when(has_down)(start_down)

    def push_w(zb, jb, own=False):
        both(
            lambda: w_copy(zb, jb, ws_up, up, own).start(),
            lambda: w_copy(zb, jb, ws_dn, down, own).start(),
        )

    for m in range(1, T):
        f_copy(m).start()
    for m in range(1, J):
        w_exchange(m).start()
    push_w(z, j, own=True)
    weights[pl.ds(pl.multiple_of(me * part, part), part), :] = w_blocks[j]
    features[t] = packed[...]
    for m in range(1, T):
        tb = lax.rem(t + m, T)
        send(packed, features.at[tb], fs.at[m], fr.at[tb], peer_t(m)).wait_recv()

    squares = jnp.zeros((slots, 1), jnp.float32)
    for tb in range(T):
        wide = features[tb].astype(jnp.float32)
        squares += jnp.sum(wide * wide, axis=1, keepdims=True)
    inverse = lax.rsqrt(squares / (T * width) + EPSILON)
    own_row = pl.multiple_of(j * block, block)
    for tb in range(T):
        at = slice(tb * width, (tb + 1) * width)
        wide = features[tb].astype(jnp.float32) * inverse * gain[:, at]
        tokens[pl.ds(own_row, slots), at] = wide.astype(jnp.bfloat16)
    tokens[pl.ds(pl.multiple_of(own_row + slots, 16), 16), :] = flags[...]
    for jb in range(J):
        tokens[jb * block + slots + 16 : (jb + 1) * block, :] = jnp.zeros(
            (PAD - 16, T * width), jnp.bfloat16
        )
    for m in range(1, J):
        t_copy(m).start()

    for m in range(1, J):
        jb = lax.rem(j + m, J)
        w_copy(z, jb, ws_up, up).wait_recv()
        push_w(z, jb)
    depth = J * part

    def product(zb):
        at = pl.ds(pl.multiple_of(zb * depth, depth), depth)
        return jnp.dot(tokens[:, at], weights[at, :], preferred_element_type=jnp.float32)

    def add_products(k):
        @pl.when(z - k >= 0)
        def _():
            total[...] += product(z - k)

        @pl.when(z + k < Z)
        def _():
            total[...] += product(z + k)

    half = w_out.shape[0] // 2

    def o_half(h):
        def o_copy(zb, sems, device, own=False):
            at = pl.ds(h * half, half)
            dst = outw_ref.at[zb, at]
            return send(
                w_out.at[at] if own else dst, dst, sems.at[2 * zb + h], orr.at[2 * zb + h], device
            )

        return o_copy

    o_halves = (o_half(0), o_half(1))

    def push_o(copy):
        both(
            lambda: copy(z, os_up, up, True).start(), lambda: copy(z, os_dn, down, True).start()
        )

    for k in range(1, Z):
        if k == Z - 1:
            push_o(o_halves[0])
            for m in range(1, J):
                jb = lax.rem(j + m, J)
                send(t_at(jb), t_at(jb), ts.at[m], tr.at[jb], peer_j(m)).wait_recv()
            total[...] = product(z)
            for done in range(1, k):
                add_products(done)
        for m in range(J):
            jb = lax.rem(j + m, J)

            @pl.when(z - k >= 0)
            def _():
                w_copy(z - k, jb, ws_up, up).wait_recv()

                @pl.when(has_up)
                def _():
                    w_copy(z - k, jb, ws_up, up).start()

            @pl.when(z + k < Z)
            def _():
                w_copy(z + k, jb, ws_dn, down).wait_recv()

                @pl.when(has_down)
                def _():
                    w_copy(z + k, jb, ws_dn, down).start()

    add_products(Z - 1)

    q_ref[...] = total[:, :q_cols].astype(jnp.bfloat16)

    def k_at(zb):
        return kv_ref.at[pl.ds(pl.multiple_of(zb * rows, rows), rows), :]

    kv_row = pl.multiple_of(z * rows, rows)
    kv_ref[pl.ds(kv_row, rows), :] = total[:, q_cols:].astype(jnp.bfloat16)
    for jb in range(J):
        kv_ref[pl.ds(pl.multiple_of(kv_row + jb * block + slots, 16), PAD), :] = tokens[
            jb * block + slots : (jb + 1) * block, : cols - q_cols
        ]

    def k_copy(zb, sems, device):
        return send(k_at(zb), k_at(zb), sems.at[zb], kr.at[zb], device)

    def relay(copy, k, up_sems, dn_sems):
        @pl.when(z - k >= 0)
        def _():
            copy(z - k, up_sems, up).wait_recv()

            @pl.when(has_up)
            def _():
                copy(z - k, up_sems, up).start()

        @pl.when(z + k < Z)
        def _():
            copy(z + k, dn_sems, down).wait_recv()

            @pl.when(has_down)
            def _():
                copy(z + k, dn_sems, down).start()

    both(lambda: k_copy(z, ks_up, up).start(), lambda: k_copy(z, ks_dn, down).start())
    for k in range(1, Z):
        if k == Z - 1:
            push_o(o_halves[1])
        relay(k_copy, k, ks_up, ks_dn)
    relay(o_halves[0], 1, os_up, os_dn)
    outw_ref[z] = w_out[...]

    for b in range(Z * J):
        seen[:, b * block : (b + 1) * block] = kv_ref[
            b * block + slots : b * block + slots + 16, :block
        ].astype(jnp.float32)
    key_pos = lax.broadcasted_iota(jnp.int32, (slots, Z * rows), 1)
    row_pos = lax.broadcasted_iota(jnp.int32, (slots, Z * rows), 0)

    @pl.loop(0, J)
    def _(jb):
        top = pl.multiple_of(jb * block, block)
        out_top = pl.multiple_of(jb * slots, 16)
        visible = (seen[0:1, :] > 0) & (key_pos <= row_pos + z * rows + top)
        for g in range(q_cols // HD):
            at = slice(g * HD, (g + 1) * HD)
            scores = lax.dot_general(
                q_ref[pl.ds(top, slots), at],
                kv_ref[:, :HD],
                (((1,), (1,)), ((), ())),
                preferred_element_type=jnp.float32,
            ) * HD ** (-0.5)
            scores = jnp.where(visible, scores, MASKED_SCORE)
            expons = jnp.exp(scores - jnp.max(scores, axis=1, keepdims=True))
            row_total = jnp.sum(expons, axis=1, keepdims=True)
            weighted = jnp.dot(
                expons.astype(jnp.bfloat16), kv_ref[:, HD:], preferred_element_type=jnp.float32
            )
            heads[j, pl.ds(out_top, slots), at] = (weighted / row_total).astype(jnp.bfloat16)

    def h_copy(m):
        return send(heads.at[j], heads.at[j], hs.at[m], hr.at[j], peer_j(m))

    for m in range(1, J):
        h_copy(m).start()
    relay(o_halves[1], 1, os_up, os_dn)
    if Z > 2:
        relay(o_halves[0], 2, os_up, os_dn)
    for m in range(1, J):
        jb = lax.rem(j + m, J)
        send(heads.at[jb], heads.at[jb], hs.at[m], hr.at[jb], peer_j(m)).wait_recv()

    def m_copy(zb, m):
        to = lax.rem(j + m, J)
        return send(
            terms.at[zb * J + to], mine.at[zb * J + j], ms.at[zb * J + m], mr.at[zb * J + j], peer_j(m)
        )

    def emit(zb):
        result = None
        for jb in range(J):
            term = jnp.dot(
                heads[jb],
                outw_ref[zb, jb * q_cols : (jb + 1) * q_cols, :],
                preferred_element_type=jnp.float32,
            )
            result = term if result is None else result + term
        rounded = result.astype(jnp.bfloat16)
        for jb in range(J):
            terms[zb * J + jb] = rounded[jb * slots : (jb + 1) * slots]
        for m in range(1, J):
            m_copy(zb, m).start()
        mine[zb * J + j] = terms[zb * J + j]

    share = Z // T

    def y_copy(zb):
        to = zb // share
        return send(
            mine.at[pl.ds(zb * J, J)],
            other.at[t, pl.ds(lax.rem(zb, share) * J, J)],
            ys.at[zb],
            yr.at[t * share + lax.rem(zb, share)],
            (me, to),
        )

    def collect(zb):
        for m in range(1, J):
            jb = lax.rem(j + m, J)
            send(
                terms.at[zb * J + jb], mine.at[zb * J + jb], ms.at[zb * J + m], mr.at[zb * J + jb], peer_j(m)
            ).wait_recv()

        @pl.when(zb // share != t)
        def _():
            y_copy(zb).start()

    def steps(k, act):
        if k == 0:
            act(z)
        else:
            pl.when(z - k >= 0)(lambda: act(z - k))
            pl.when(z + k < Z)(lambda: act(z + k))

    steps(0, emit)
    for k in range(1, Z):
        if k > 1:
            relay(o_halves[1], k, os_up, os_dn)
            if k + 1 < Z:
                relay(o_halves[0], k + 1, os_up, os_dn)
        steps(k, emit)
        steps(k - 1, collect)
    steps(Z - 1, collect)

    for m in range(1, T):
        tb = lax.rem(t + m, T)
        for zl in range(share):
            at = pl.ds(zl * J, J)
            send(
                mine.at[at], other.at[tb, at], ys.at[zl], yr.at[tb * share + zl], peer_t(m)
            ).wait_recv()
    for b in range(share * J):
        owned = mine[t * share * J + b].astype(jnp.float32)
        for m in range(1, T):
            owned += other[lax.rem(t + m, T), b].astype(jnp.float32)
        mixed_ref[:, b * part : (b + 1) * part] = owned.astype(jnp.bfloat16)

    for m in range(1, T):
        f_copy(m).wait_send()
    for m in range(1, J):
        w_exchange(m).wait_send()
        t_copy(m).wait_send()
        h_copy(m).wait_send()
    for zb in range(Z):
        for m in range(1, J):
            m_copy(zb, m).wait_send()

        @pl.when(zb // share != t)
        def _():
            y_copy(zb).wait_send()

        for up_way, sems_of, device in ((True, (ws_up, ks_up, os_up), up), (False, (ws_dn, ks_dn, os_dn), down)):
            sent = has_up & (zb <= z) if up_way else has_down & (zb >= z)

            @pl.when(sent)
            def _():
                for jb in range(J):
                    w_copy(zb, jb, sems_of[0], device).wait_send()
                k_copy(zb, sems_of[1], device).wait_send()
                for copy in o_halves:
                    copy(zb, sems_of[2], device).wait_send()


def gathered(J, Z, T, packed, flags, gain, w_blocks, w_out):
    slots, width = packed.shape
    part, cols = w_blocks.shape[1:]
    rows = J * LANES
    q_cols = cols - 2 * HD
    vmem = pl.BlockSpec(memory_space=pltpu.VMEM)
    dma = pltpu.SemaphoreType.DMA
    bf16 = jnp.bfloat16
    return pl.pallas_call(
        functools.partial(gather_kernel, J, Z, T),
        out_shape=jax.ShapeDtypeStruct((slots, width), bf16),
        in_specs=[vmem] * 5,
        out_specs=vmem,
        scratch_shapes=[
            pltpu.VMEM((rows, q_cols), bf16),
            pltpu.VMEM((Z * rows, 2 * HD), bf16),
            pltpu.VMEM((Z,) + w_out.shape, bf16),
            pltpu.VMEM((T, slots, width), bf16),
            pltpu.VMEM((rows, T * width), bf16),
            pltpu.VMEM((T * width, cols), bf16),
            pltpu.VMEM((rows, cols), jnp.float32),
            pltpu.VMEM((16, Z * rows), jnp.float32),
            pltpu.VMEM((J, J * slots, q_cols), bf16),
            pltpu.VMEM((Z * J, slots, w_out.shape[1]), bf16),
            pltpu.VMEM((Z * J, slots, w_out.shape[1]), bf16),
            pltpu.VMEM((T, Z // T * J, slots, w_out.shape[1]), bf16),
            dma((J,)), dma((J,)), dma((T,)), dma((T,)), dma((J,)), dma((J,)),
            dma((Z * J,)), dma((Z * J,)), dma((Z * J,)),
            dma((Z,)), dma((Z,)), dma((Z,)), dma((2 * Z,)), dma((2 * Z,)), dma((2 * Z,)),
            dma((J,)), dma((J,)), dma((Z * J,)), dma((Z * J,)), dma((Z,)), dma((Z,)),
        ],
        compiler_params=pltpu.CompilerParams(
            collective_id=0, has_side_effects=True, vmem_limit_bytes=48 * 1024 * 1024
        ),
    )(packed, flags, gain, w_blocks, w_out)


def body(n_seq, n_tensor, hidden, depth, norm_gain, w_query, w_key, w_value, w_out):
    rows, width = hidden.shape
    slots = rows // 2
    d_model = width * n_tensor
    kv_heads = w_key.shape[1] // HD
    group = w_query.shape[1] // w_key.shape[1]
    J = kv_heads
    Z = n_seq // J
    part = w_query.shape[0]
    head_cols = (group + 2) * HD
    me = lax.axis_index("seq")
    t = lax.axis_index("tensor")
    j = lax.rem(me, J)
    z = me // J
    z_groups = [[a * J + b for a in range(Z)] for b in range(J)]

    def shift_j(value, k):
        pairs = [(a * J + b, a * J + (b + k) % J) for a in range(Z) for b in range(J)]
        return lax.ppermute(value, "seq", pairs)

    def shift_t(value, k):
        return lax.ppermute(value, "tensor", [(b, (b + k) % n_tensor) for b in range(n_tensor)])

    def gather_z(value, axis):
        return lax.all_gather(value, "seq", axis=axis, tiled=True, axis_index_groups=z_groups)

    def gather_j(value):
        return [value] + [shift_j(value, J - m) for m in range(1, J)]

    def exchange_j(block_for):
        return [block_for(j)] + [
            shift_j(block_for(lax.rem(j + J - m, J)), J - m) for m in range(1, J)
        ]

    living = depth > STEP
    index = jnp.arange(rows, dtype=jnp.int32)
    rank = jnp.sum(
        jnp.where(living[None, :] & (index[None, :] <= index[:, None]), 1, 0), axis=1
    ) - 1
    slot_ids = jnp.arange(slots, dtype=jnp.int32)
    select = (living[None, :] & (rank[None, :] == slot_ids[:, None])).astype(jnp.bfloat16)
    filled = jnp.sum(select.astype(jnp.float32), axis=1).astype(jnp.bfloat16)
    packed = jnp.dot(select, hidden, preferred_element_type=jnp.float32).astype(jnp.bfloat16)

    def columns_of(i):
        return jnp.concatenate(
            [
                lax.dynamic_slice_in_dim(w_query, i * group * HD, group * HD, axis=1),
                lax.dynamic_slice_in_dim(w_key, i * HD, HD, axis=1),
                lax.dynamic_slice_in_dim(w_value, i * HD, HD, axis=1),
            ],
            axis=1,
        )

    fast = 1 < Z <= 8 and J > 1 and n_tensor > 1 and slots % 16 == 0 and slots < LANES - 16 and Z % n_tensor == 0 and part == w_out.shape[1]
    fast = fast and w_out.shape[1] % 128 == 0 and part % 16 == 0
    if fast:
        flag_rows = jnp.broadcast_to(
            jnp.pad(filled, (0, d_model - slots))[None, :], (16, d_model)
        )
        w_blocks = jnp.stack([columns_of(i) for i in range(J)])
        mixed = gathered(J, Z, n_tensor, packed, flag_rows, norm_gain[None, :], w_blocks, w_out)
        return jnp.einsum(
            "sr,sf->rf", select, mixed, preferred_element_type=jnp.float32
        ).astype(jnp.bfloat16)

    w_rows = rolled(exchange_j(columns_of), 0, j)
    weights = gather_z(w_rows, 0)
    out_rows = group * HD
    twice = jnp.concatenate([w_out, w_out], axis=0) if J > 1 else w_out
    w_out_turned = lax.dynamic_slice_in_dim(twice, j * out_rows, J * out_rows, axis=0)
    out_weights = gather_z(w_out_turned, 1)

    features = rolled([packed] + [shift_t(packed, n_tensor - m) for m in range(1, n_tensor)], 1, t)
    widened = features.astype(jnp.float32)
    inverse = lax.rsqrt(jnp.mean(widened * widened, axis=1, keepdims=True) + EPSILON)
    normed = (widened * inverse * norm_gain[None, :]).astype(jnp.bfloat16)
    block_rows = J * slots
    tokens = jnp.concatenate(gather_j(normed), axis=0)
    flags = jnp.concatenate(gather_j(filled), axis=0)

    qkv = jnp.dot(tokens, weights, preferred_element_type=jnp.float32).astype(jnp.bfloat16)
    queries = qkv[:, : group * HD].reshape(block_rows, group, HD)
    kv = qkv[:, group * HD :]
    flag_rows = -(-block_rows // (2 * HD))
    flag_pad = -(-flag_rows // 16) * 16
    flag_block = jnp.pad(flags, (0, flag_pad * 2 * HD - block_rows)).reshape(flag_pad, 2 * HD)
    arrived = gather_z(jnp.concatenate([kv, flag_block], axis=0), 0).reshape(
        Z, block_rows + flag_pad, 2 * HD
    )
    keys = arrived[:, :block_rows, :HD].reshape(Z * block_rows, HD)
    values = arrived[:, :block_rows, HD:].reshape(Z * block_rows, HD)
    key_flags = arrived[:, block_rows:].reshape(Z, -1)[:, :block_rows].reshape(Z * block_rows)

    local = jnp.arange(block_rows, dtype=jnp.int32)
    turned = lax.rem(local // slots + j, J) * slots + lax.rem(local, slots)
    query_pos = z * block_rows + turned
    key_pos = (jnp.arange(Z, dtype=jnp.int32)[:, None] * block_rows + turned[None, :]).reshape(-1)
    visible = (key_flags[None, :] > 0) & (key_pos[None, :] <= query_pos[:, None])
    scores = jnp.einsum(
        "qgd,kd->gqk", queries, keys, preferred_element_type=jnp.float32
    ) * HD ** (-0.5)
    scores = jnp.where(visible[None], scores, MASKED_SCORE)
    expons = jnp.exp(scores - jnp.max(scores, axis=-1, keepdims=True))
    total = jnp.sum(expons, axis=-1)
    weighted = jnp.einsum(
        "gqk,kd->gqd", expons.astype(jnp.bfloat16), values, preferred_element_type=jnp.float32
    )
    attended = (weighted / total[..., None]).astype(jnp.bfloat16)
    attended = jnp.transpose(attended, (1, 0, 2)).reshape(block_rows, group * HD)
    attended = rolled([attended[m * slots : (m + 1) * slots] for m in range(J)], 0, j)
    heads = jnp.concatenate(gather_j(attended), axis=1)
    terms = jnp.dot(heads, out_weights, preferred_element_type=jnp.float32).astype(jnp.bfloat16)
    own_cols = w_out.shape[1]
    mine = exchange_j(lambda i: lax.dynamic_slice_in_dim(terms, i * slots, slots, axis=0))
    mine = [piece.reshape(slots, Z, 1, own_cols) for piece in mine]
    mine = rolled(mine, 2, j).reshape(slots, d_model)

    def features_of(i):
        return lax.dynamic_slice_in_dim(mine, i * width, width, axis=1)

    owned = features_of(t).astype(jnp.float32)
    for k in range(1, n_tensor):
        owned = owned + shift_t(features_of(lax.rem(t + k, n_tensor)), k).astype(jnp.float32)
    mixed = owned.astype(jnp.bfloat16)
    return jnp.einsum(
        "sr,sf->rf", select, mixed, preferred_element_type=jnp.float32
    ).astype(jnp.bfloat16)


def solution(mesh):
    n_seq, n_tensor = mesh.shape["seq"], mesh.shape["tensor"]

    def step(*args):
        return body(n_seq, n_tensor, *args)

    return jax.shard_map(
        step,
        mesh=mesh,
        in_specs=(
            P("seq", "tensor"),
            P("seq"),
            P(),
            P("seq", "tensor"),
            P("seq", "tensor"),
            P("seq", "tensor"),
            P("tensor", "seq"),
        ),
        out_specs=P("seq", "tensor"),
        check_vma=False,
    )
```
